256 devices in a mesh: word: 16 (over z_lo, x, core), ctx: 16 (over y, z_hi).
Axes of the slice: x: 4, y: 4, z: 8 (z_hi: 4, z_lo: 2; z = z_hi * 2 + z_lo), core: 2. Of those that a mesh axis runs over, the one named last changes fastest.
Arguments:
- counts: int32 [24576, 24576], P('word', 'ctx'), may hold values from 0 to 1800, as said below
- word_vecs: float32 [24576, 300], P(('word', 'ctx')), may hold values from -0.35 to 0.35
- word_bias: float32 [24576], P(('word', 'ctx')), may hold values from 0.5 to 3
- word_accum: float32 [24576, 300], P(('word', 'ctx')), may hold values from 1.6276042e-06 to 8.138021e-05
- word_bias_accum: float32 [24576], P(('word', 'ctx')), may hold values from 1 to 30
- ctx_vecs: float32 [24576, 300], P(('ctx', 'word')), may hold values from -0.35 to 0.35
- ctx_bias: float32 [24576], P(('ctx', 'word')), may hold values from 0.5 to 3
- ctx_accum: float32 [24576, 300], P(('ctx', 'word')), may hold values from 1.6276042e-06 to 8.138021e-05
- ctx_bias_accum: float32 [24576], P(('ctx', 'word')), may hold values from 1 to 30
Outputs:
- new_word_vecs: float32 [24576, 300], P(('word', 'ctx'))
- new_word_bias: float32 [24576], P(('word', 'ctx'))
- new_word_accum: float32 [24576, 300], P(('word', 'ctx'))
- new_word_bias_accum: float32 [24576], P(('word', 'ctx'))
- new_ctx_vecs: float32 [24576, 300], P(('ctx', 'word'))
- new_ctx_bias: float32 [24576], P(('ctx', 'word'))
- new_ctx_accum: float32 [24576, 300], P(('ctx', 'word'))
- new_ctx_bias_accum: float32 [24576], P(('ctx', 'word'))
The draws below stay inside these ranges and needn't reach their ends.
Inputs may be any that keep to these rules, and one draw needn't show every extreme that they name: counts are non-negative integers, and a count is zero exactly where the word and the context never co-occur.
All inputs are finite; a program needn't handle non-finite values.
Results may differ from the reference program's by a relative error of at most 0.0045.
Values may be sent and summed in bfloat16 or wider, within the bound.
No kernel may reach another device: no remote copies, remote signals or barrier semaphores. Data moves between devices by JAX's collectives and lax.ppermute only.
A program may use at most 64 MiB of HBM per device.

```python
import math
import jax
import jax.numpy as jnp
from jax import lax

D = 300
TW = 1536
WORDS = 24576
CONTEXTS = 24576


def draw_counts(key, part):
    key_scale = jax.random.fold_in(key, 11)
    key_value = jax.random.fold_in(key, 23)
    key_empty = jax.random.fold_in(key, 37)
    shape = (WORDS, CONTEXTS)
    exponent = jax.random.randint(key_scale, shape, 0, 12)
    upper = jnp.left_shift(jnp.ones(shape, jnp.int32), exponent) + 1
    values = jnp.minimum(jax.random.randint(key_value, shape, 1, upper), 1800)
    empty = jax.random.randint(key_empty, shape, 0, 8) == 0
    drawn = jnp.where(empty, 0, values)
    rows = jnp.arange(WORDS, dtype=jnp.int32)[:, None]
    cols = jnp.arange(CONTEXTS, dtype=jnp.int32)[None, :]
    corner = (rows == 0) & (cols == 0)
    return jnp.where(corner, 1800, drawn).astype(jnp.int32)


def draw_word_vecs(key, part):
    key_entries = jax.random.fold_in(key, 43)
    entries = 0.1 * jax.random.normal(key_entries, (WORDS, D), jnp.float32)
    return jnp.clip(entries, -0.35, 0.35).astype(jnp.float32)


def draw_ctx_vecs(key, part):
    key_entries = jax.random.fold_in(key, 59)
    entries = 0.1 * jax.random.normal(key_entries, (CONTEXTS, D), jnp.float32)
    return jnp.clip(entries, -0.35, 0.35).astype(jnp.float32)


def steps_of(stream_key, dims, pieces, least, top_value):
    def one(dim, parts):
        heights = jax.random.uniform(jax.random.fold_in(jax.random.fold_in(stream_key, 6), dim), (parts,), jnp.float32, least / len(pieces), top_value / len(pieces))
        return jnp.repeat(jnp.exp(heights), dims[dim] // parts).reshape((-1,) + (1,) * (len(dims) - dim - 1))

    factor_of = one(*pieces[0])
    for cut in pieces[1:]:
        factor_of = factor_of * one(*cut)
    return factor_of


def setup_inputs(seed: int = 0) -> dict:
    arg_keys = jax.random.split(jax.random.key(seed), 10)
    return {
        "counts": draw_counts(jax.random.fold_in(arg_keys[9], 71), 0),
        "word_vecs": draw_word_vecs(jax.random.fold_in(arg_keys[9], 71), 0),
        "word_bias": jnp.clip(0.5 + 2.5 * jax.random.uniform(arg_keys[2], (WORDS,), jnp.float32) ** steps_of(arg_keys[2], (WORDS,), ((0, 256),), -0.2, 0.2), 0.5, 3.0),
        "word_accum": jnp.clip(jnp.exp(math.log(8.138021075865254e-05) - 3.912023 * jax.random.uniform(arg_keys[3], (WORDS, D), jnp.float32) ** steps_of(arg_keys[3], (WORDS, D), ((0, 256),), -0.2, 0.2)), 1.6276042060781037e-06, 8.138021075865254e-05),
        "word_bias_accum": jnp.clip(jnp.exp(math.log(30.0) - 3.4011974 * jax.random.uniform(arg_keys[4], (WORDS,), jnp.float32) ** steps_of(arg_keys[4], (WORDS,), ((0, 256),), -0.2, 0.2)), 1.0, 30.0),
        "ctx_vecs": draw_ctx_vecs(jax.random.fold_in(arg_keys[9], 71), 0),
        "ctx_bias": jnp.clip(0.5 + 2.5 * jax.random.uniform(arg_keys[6], (CONTEXTS,), jnp.float32) ** steps_of(arg_keys[6], (CONTEXTS,), ((0, 256),), -0.2, 0.2), 0.5, 3.0),
        "ctx_accum": jnp.clip(jnp.exp(math.log(8.138021075865254e-05) - 3.912023 * jax.random.uniform(arg_keys[7], (CONTEXTS, D), jnp.float32) ** steps_of(arg_keys[7], (CONTEXTS, D), ((0, 256),), -0.2, 0.2)), 1.6276042060781037e-06, 8.138021075865254e-05),
        "ctx_bias_accum": jnp.clip(jnp.exp(math.log(30.0) - 3.4011974 * jax.random.uniform(arg_keys[8], (CONTEXTS,), jnp.float32) ** steps_of(arg_keys[8], (CONTEXTS,), ((0, 256),), -0.2, 0.2)), 1.0, 30.0),
    }


count_cap = 100.0
power_law = 0.75
step_rate = 0.2

def weighted_residual(tile_counts, word_rows, ctx_rows, word_bias_rows, ctx_bias_rows):
    values = tile_counts.astype(jnp.float32)
    log_count = jnp.log(jnp.maximum(values, 1.0))
    weight = jnp.where(tile_counts > 0, jnp.minimum((values / count_cap) ** power_law, 1.0), 0.0)
    inner = lax.dot_general(word_rows, ctx_rows, (((1,), (1,)), ((), ())), preferred_element_type=jnp.float32)
    return weight * (inner + word_bias_rows[:, None] + ctx_bias_rows[None, :] - log_count)

def adagrad(param, accum, grad):
    new_accum = accum + grad * grad
    return (param - step_rate * grad / jnp.sqrt(new_accum), new_accum)

def reference(counts, word_vecs, word_bias, word_accum, word_bias_accum, ctx_vecs, ctx_bias, ctx_accum, ctx_bias_accum):
    word_low = word_vecs.astype(jnp.bfloat16)
    ctx_low = ctx_vecs.astype(jnp.bfloat16)
    word_bias_f = lax.optimization_barrier(word_bias.astype(jnp.bfloat16)).astype(jnp.float32)
    ctx_bias_f = lax.optimization_barrier(ctx_bias.astype(jnp.bfloat16)).astype(jnp.float32)
    groups = WORDS // TW
    count_blocks = counts.reshape(groups, TW, CONTEXTS)
    word_blocks = word_low.reshape(groups, TW, D)
    bias_blocks = word_bias_f.reshape(groups, TW)

    def one_block(carry, inputs):
        ctx_total, ctx_bias_total = carry
        block_counts, block_words, block_bias = inputs
        scaled = weighted_residual(block_counts, block_words, ctx_low, block_bias, ctx_bias_f)
        scaled_low = scaled.astype(jnp.bfloat16)
        word_term = jnp.dot(scaled_low, ctx_low, preferred_element_type=jnp.float32)
        word_bias_term = lax.optimization_barrier(jnp.sum(scaled, axis=1))
        ctx_term = lax.dot_general(scaled_low, block_words, (((0,), (0,)), ((), ())), preferred_element_type=jnp.float32)
        return ((ctx_total + ctx_term, ctx_bias_total + lax.optimization_barrier(jnp.sum(scaled, axis=0))), (word_term, word_bias_term))
    start = (jnp.zeros((CONTEXTS, D), jnp.float32), jnp.zeros((CONTEXTS,), jnp.float32))
    (ctx_sum, ctx_bias_sum), (word_sum, word_bias_sum) = lax.scan(one_block, start, (count_blocks, word_blocks, bias_blocks))
    word_grad = 2.0 / CONTEXTS * word_sum.reshape(WORDS, D)
    word_bias_grad = 2.0 / CONTEXTS * word_bias_sum.reshape(WORDS)
    ctx_grad = 2.0 / WORDS * ctx_sum
    ctx_bias_grad = 2.0 / WORDS * ctx_bias_sum
    new_word_vecs, new_word_accum = adagrad(word_vecs, word_accum, word_grad)
    new_word_bias, new_word_bias_accum = adagrad(word_bias, word_bias_accum, word_bias_grad)
    new_ctx_vecs, new_ctx_accum = adagrad(ctx_vecs, ctx_accum, ctx_grad)
    new_ctx_bias, new_ctx_bias_accum = adagrad(ctx_bias, ctx_bias_accum, ctx_bias_grad)
    return (new_word_vecs, new_word_bias, new_word_accum, new_word_bias_accum, new_ctx_vecs, new_ctx_bias, new_ctx_accum, new_ctx_bias_accum)
```

```python
import functools

import jax
import jax.numpy as jnp
from jax import lax
from jax.experimental import pallas as pl
from jax.experimental.pallas import tpu as pltpu
from jax.sharding import PartitionSpec as P


count_cap = 100.0
power_law = 0.75
step_rate = 0.2

ROWS = 96
BLOCK = 120
HALF = 64
D = 300
LO = 256
MIB = 1 << 20


def pack_rows(main, tail):
    lane = lax.broadcasted_iota(jnp.int32, (24, 128), 1)
    low = lane < 64
    t = [tail[24 * g : 24 * g + 24, :] for g in range(4)]
    left = jnp.where(low, t[0], pltpu.roll(t[1], 64, 1))
    right = jnp.where(low, t[2], pltpu.roll(t[3], 64, 1))
    return jnp.concatenate([main, jnp.concatenate([left, right], axis=1)], axis=0)


def unpack_tail(packed):
    left, right = packed[ROWS:BLOCK, :128], packed[ROWS:BLOCK, 128:]
    return jnp.concatenate([left, pltpu.roll(left, 64, 1), right, pltpu.roll(right, 64, 1)], axis=0)


def to_column(row):
    eye = lax.broadcasted_iota(jnp.int32, (ROWS, ROWS), 0) == lax.broadcasted_iota(jnp.int32, (ROWS, ROWS), 1)
    return jnp.sum(jnp.where(eye, jnp.broadcast_to(row, (ROWS, ROWS)), 0.0), axis=1, keepdims=True)


def to_row(column):
    eye = lax.broadcasted_iota(jnp.int32, (ROWS, ROWS), 0) == lax.broadcasted_iota(jnp.int32, (ROWS, ROWS), 1)
    return jnp.sum(jnp.where(eye, jnp.broadcast_to(column, (ROWS, ROWS)), 0.0), axis=0, keepdims=True)


def pack_kernel(bias_lane, vec_ref, bias_ref, out_ref, tail_ref):
    tail_ref[...] = jnp.zeros_like(tail_ref)
    tail_ref[:, : D - LO] = vec_ref[:, LO:]
    lane = lax.broadcasted_iota(jnp.int32, (ROWS, 128), 1)
    tail = jnp.where(lane == bias_lane, jnp.broadcast_to(to_column(bias_ref[...]), (ROWS, 128)), tail_ref[...])
    out_ref[...] = pack_rows(vec_ref[:, :LO], tail).astype(jnp.bfloat16)


def pack(vecs, bias, bias_lane, name):
    return pl.pallas_call(
        functools.partial(pack_kernel, bias_lane),
        out_shape=jax.ShapeDtypeStruct((BLOCK, LO), jnp.bfloat16),
        scratch_shapes=[pltpu.VMEM((ROWS, 128), jnp.float32)],
        compiler_params=pltpu.CompilerParams(vmem_limit_bytes=4 * MIB),
        cost_estimate=pl.CostEstimate(flops=100000, bytes_accessed=200000, transcendentals=0),
        name=name,
    )(vecs, bias.reshape(1, ROWS))


def weight_kernel(index_ref, counts_ref, weight_ref, log_ref):
    counts = counts_ref[...]
    values = counts.astype(jnp.float32)
    log_count = jnp.log(jnp.maximum(values, 1.0))
    power = jnp.exp(jnp.minimum(power_law * (log_count - jnp.log(jnp.float32(count_cap))), 0.0))
    weight_ref[...] = jnp.where(counts > 0, power, 0.0)
    log_ref[...] = log_count


def weights(index, counts, name):
    rows, columns = 4 * ROWS, counts.shape[1]
    spec = pl.BlockSpec((ROWS, columns), lambda j, index: (j, 0))
    return pl.pallas_call(
        weight_kernel,
        grid_spec=pltpu.PrefetchScalarGridSpec(
            num_scalar_prefetch=1,
            grid=(4,),
            in_specs=[pl.BlockSpec((ROWS, columns), lambda j, index: (index[j], 0))],
            out_specs=[spec, spec],
        ),
        out_shape=[jax.ShapeDtypeStruct((rows, columns), jnp.float32)] * 2,
        compiler_params=pltpu.CompilerParams(vmem_limit_bytes=6 * MIB),
        cost_estimate=pl.CostEstimate(
            flops=20 * rows * columns, bytes_accessed=12 * rows * columns, transcendentals=2 * rows * columns
        ),
        name=name,
    )(index, counts)


def tile_kernel(
    index_ref, w0, w1, w2a, w2b, w3, c0, c1, k0, l0, k1, l1, k2, l2, k3, l3,
    g0, g1, g2a, g2b, g3, h_own, h_other,
    words, ctx_full, ctx_t, ctx_grad, back,
):
    lane = lax.broadcasted_iota(jnp.int32, (ROWS, 128), 1)
    bw, bc = D - LO, D - LO + 1

    def rows_of(i):
        return pl.ds(pl.multiple_of(index_ref[i] * ROWS, ROWS), ROWS)

    for i in range(16):
        packed = (c0 if i < 8 else c1)[i % 8].astype(jnp.float32)
        tail = unpack_tail(packed)
        tail = jnp.where(lane == bw, 1.0, jnp.where(lane <= bc, tail, 0.0))
        ctx_full[rows_of(i), :LO] = packed[:ROWS].astype(jnp.bfloat16)
        ctx_full[rows_of(i), LO:] = tail.astype(jnp.bfloat16)
    ctx_t[...] = ctx_full[...].T

    for k, (sources, weight, log_count) in enumerate(
        (((w0,), k0, l0), ((w1,), k1, l1), ((w2a, w2b), k2, l2), ((w3,), k3, l3))
    ):
        for j in range(4):
            ref = sources[0] if len(sources) == 1 else sources[j // 2]
            packed = ref[j if len(sources) == 1 else j % 2].astype(jnp.float32)
            tail = unpack_tail(packed)
            tail = jnp.where(lane < bc, tail, jnp.where(lane == bc, 1.0, 0.0))
            words[ROWS * j : ROWS * j + ROWS, :LO] = packed[:ROWS].astype(jnp.bfloat16)
            words[ROWS * j : ROWS * j + ROWS, LO:] = tail.astype(jnp.bfloat16)
        word_rows = words[...]
        inner = jnp.dot(word_rows, ctx_t[...], preferred_element_type=jnp.float32)
        scaled = (weight[...] * (inner - log_count[...])).astype(jnp.bfloat16)
        word_term = jnp.dot(scaled, ctx_full[...], preferred_element_type=jnp.float32)
        for j in range(4):
            term = word_term[ROWS * j : ROWS * j + ROWS]
            packed = pack_rows(term[:, :LO], term[:, LO:])
            if k == 0:
                g0[j] = packed
            elif k == 1:
                g1[j] = packed
            elif k == 3:
                g3[j] = packed
            else:
                (g2a, g2b)[j // 2][j % 2] = packed.astype(jnp.bfloat16)
        ctx_term = jnp.dot(word_rows.T, scaled, preferred_element_type=jnp.float32)
        ctx_grad[...] = ctx_term if k == 0 else ctx_grad[...] + ctx_term

    back[...] = ctx_grad[...].T
    for i in range(16):
        term = back[rows_of(i), :]
        packed = pack_rows(term[:, :LO], term[:, LO:])
        if i < 8:
            h_own[i] = packed
        else:
            h_other[i - 8] = packed.astype(jnp.bfloat16)


def tile_gradients(index, word_parts, ctx_parts, weighted):
    columns = 16 * ROWS
    f32, low = jnp.float32, jnp.bfloat16
    shape = lambda n, t: jax.ShapeDtypeStruct((n, BLOCK, LO), t)
    vmem = pl.BlockSpec(memory_space=pltpu.VMEM)
    operands = (*word_parts, *ctx_parts, *weighted)
    return pl.pallas_call(
        tile_kernel,
        in_specs=[pl.BlockSpec(memory_space=pltpu.SMEM)] + [vmem] * len(operands),
        out_specs=[vmem] * 7,
        out_shape=[shape(4, f32), shape(4, f32), shape(2, low), shape(2, low), shape(4, f32), shape(8, f32), shape(8, low)],
        scratch_shapes=[
            pltpu.VMEM((4 * ROWS, 384), low),
            pltpu.VMEM((columns, 384), low),
            pltpu.VMEM((384, columns), low),
            pltpu.VMEM((384, columns), f32),
            pltpu.VMEM((columns, 384), f32),
        ],
        compiler_params=pltpu.CompilerParams(vmem_limit_bytes=44 * MIB),
        cost_estimate=pl.CostEstimate(flops=6 * columns * columns * 384, bytes_accessed=24 * MIB, transcendentals=0),
        name="tile",
    )(index, *operands)


def update_kernel(bias_lane, scale, total_ref, add_a, add_b, vec_ref, bias_ref, acc_ref, bacc_ref, nv, nb, na, nba):
    packed = total_ref[...] + add_a[...].astype(jnp.float32)
    if add_b is not None:
        packed = packed + add_b[...].astype(jnp.float32)
    packed = packed * scale
    tail = unpack_tail(packed)
    for columns, grad in ((slice(0, LO), packed[:ROWS]), (slice(LO, D), tail[:, : D - LO])):
        accum = acc_ref[:, columns] + grad * grad
        na[:, columns] = accum
        nv[:, columns] = vec_ref[:, columns] - step_rate * grad / jnp.sqrt(accum)
    grad = to_row(tail[:, bias_lane : bias_lane + 1])
    accum = bacc_ref[...] + grad * grad
    nba[...] = accum
    nb[...] = bias_ref[...] - step_rate * grad / jnp.sqrt(accum)


def update(total, add_a, add_b, vecs, bias, accum, bias_accum, bias_lane, scale, name):
    row = lambda a: a.reshape(1, ROWS)
    if add_b is None:
        kernel = lambda t, a, *rest: update_kernel(bias_lane, scale, t, a, None, *rest)
        sums = (total, add_a)
    else:
        kernel = functools.partial(update_kernel, bias_lane, scale)
        sums = (total, add_a, add_b)
    f32 = jnp.float32
    nv, nb, na, nba = pl.pallas_call(
        kernel,
        out_shape=[
            jax.ShapeDtypeStruct((ROWS, D), f32),
            jax.ShapeDtypeStruct((1, ROWS), f32),
            jax.ShapeDtypeStruct((ROWS, D), f32),
            jax.ShapeDtypeStruct((1, ROWS), f32),
        ],
        compiler_params=pltpu.CompilerParams(vmem_limit_bytes=6 * MIB),
        cost_estimate=pl.CostEstimate(flops=400000, bytes_accessed=800000, transcendentals=30000),
        name=name,
    )(*sums, vecs, row(bias), accum, row(bias_accum))
    return nv, nb.reshape(ROWS), na, nba.reshape(ROWS)


def ctx_shift(value, dy, dz):
    perm = [(i, ((i // 4 + dy) % 4) * 4 + (i % 4 + dz) % 4) for i in range(16)]
    return lax.ppermute(value, "ctx", perm)


def word_shift(value, dl, dx, dc):
    perm = [(i, ((i // 8 + dl) % 2) * 8 + ((i // 2 % 4 + dx) % 4) * 2 + (i % 2 + dc) % 2) for i in range(16)]
    return lax.ppermute(value, "word", perm)


def per_device(
    counts,
    word_vecs,
    word_bias,
    word_accum,
    word_bias_accum,
    ctx_vecs,
    ctx_bias,
    ctx_accum,
    ctx_bias_accum,
):
    f32, low = jnp.float32, jnp.bfloat16
    p = lax.axis_index("ctx").astype(jnp.int32)
    y, z = p // 4, p % 4
    q = lax.axis_index("word").astype(jnp.int32)
    zl, x, c = q // 8, q // 2 % 4, q % 2

    word_block = pack(word_vecs, word_bias, D - LO, "pack_word")
    ctx_block = pack(ctx_vecs, ctx_bias, D - LO + 1, "pack_ctx")

    zm, zp = ctx_shift(word_block, 0, 1), ctx_shift(word_block, 0, -1)
    pair = jnp.stack([ctx_block, word_shift(ctx_block, 1, 0, 0)])
    zoa, zob = ctx_shift(zm[:HALF], 0, 1), ctx_shift(zp[HALF:], 0, -1)
    xm, xp = word_shift(pair, 0, 1, 0), word_shift(pair, 0, -1, 0)
    w0 = jnp.stack([word_block, zp, jnp.concatenate([zoa, zob]), zm])
    w3, w1 = ctx_shift(w0, 1, 0), ctx_shift(w0, -1, 0)
    xoa, xob = word_shift(xm[:1], 0, 1, 0), word_shift(xp[1:], 0, -1, 0)
    c0 = jnp.concatenate([pair, xp, xm, xoa, xob])
    c1 = word_shift(c0, 0, 0, 1)
    w2a, w2b = ctx_shift(w3[:2], 1, 0), ctx_shift(w1[2:], -1, 0)

    step = jnp.arange(4, dtype=jnp.int32)
    weighted = []
    for k in range(4):
        weighted += weights((y + k) % 4 * 4 + (z + step) % 4, counts, f"weights_{k}")

    order = [(b, a, d) for d in (0, 1) for b in (0, 1, 3, 2) for a in (0, 1)]
    bs, avs, ds = (jnp.array(v, jnp.int32) for v in zip(*order))
    index = (zl + avs) % 2 * 8 + (x + bs) % 4 * 2 + (c + ds) % 2
    g0, g1, g2a, g2b, g3, h_own, h_other = tile_gradients(index, (w0, w1, w2a, w2b, w3), (c0, c1), weighted)

    ya, yb = ctx_shift(g2a, 1, 0), ctx_shift(g2b, -1, 0)
    hc = word_shift(h_other, 0, 0, 1)
    send_p = jnp.concatenate([g1[:2] + ya.astype(f32), g1[2:]]).astype(low)
    send_m = jnp.concatenate([g3[:2], g3[2:] + yb.astype(f32)]).astype(low)
    ym, yp = ctx_shift(send_p, 1, 0), ctx_shift(send_m, -1, 0)
    s = h_own + hc.astype(f32)
    xa, xb = word_shift(s[6:7].astype(low), 0, 1, 0), word_shift(s[7:8].astype(low), 0, -1, 0)
    g = g0 + ym.astype(f32) + yp.astype(f32)
    far = g[2].astype(low)
    za, zb = ctx_shift(far[:HALF], 0, 1), ctx_shift(far[HALF:], 0, -1)
    send_xp = jnp.concatenate([s[2:3] + xa.astype(f32), s[3:4]]).astype(low)
    send_xm = jnp.concatenate([s[4:5], s[5:6] + xb.astype(f32)]).astype(low)
    rxm, rxp = word_shift(send_xp, 0, 1, 0), word_shift(send_xm, 0, -1, 0)
    send_zp = jnp.concatenate([g[1, :HALF] + za.astype(f32), g[1, HALF:]]).astype(low)
    send_zm = jnp.concatenate([g[3, :HALF], g[3, HALF:] + zb.astype(f32)]).astype(low)
    rzm, rzp = ctx_shift(send_zp, 0, 1), ctx_shift(send_zm, 0, -1)
    t = s[:2] + rxm.astype(f32) + rxp.astype(f32)
    rl = word_shift(t[1].astype(low), 1, 0, 0)

    word_scale = 2.0 / (counts.shape[1] * lax.axis_size("ctx"))
    ctx_scale = 2.0 / (counts.shape[0] * lax.axis_size("word"))
    new_word_vecs, new_word_bias, new_word_accum, new_word_bias_accum = update(
        g[0], rzm, rzp, word_vecs, word_bias, word_accum, word_bias_accum, D - LO, word_scale, "update_word"
    )
    new_ctx_vecs, new_ctx_bias, new_ctx_accum, new_ctx_bias_accum = update(
        t[0], rl, None, ctx_vecs, ctx_bias, ctx_accum, ctx_bias_accum, D - LO + 1, ctx_scale, "update_ctx"
    )
    return (
        new_word_vecs,
        new_word_bias,
        new_word_accum,
        new_word_bias_accum,
        new_ctx_vecs,
        new_ctx_bias,
        new_ctx_accum,
        new_ctx_bias_accum,
    )


def solution(mesh):
    words, contexts = P(("word", "ctx")), P(("ctx", "word"))
    return jax.shard_map(
        per_device,
        mesh=mesh,
        in_specs=(P("word", "ctx"), words, words, words, words, contexts, contexts, contexts, contexts),
        out_specs=(words, words, words, words, contexts, contexts, contexts, contexts),
        check_vma=False,
    )
```

```python
import functools

import jax
import jax.numpy as jnp
from jax import lax
from jax.experimental import pallas as pl
from jax.experimental.pallas import tpu as pltpu
from jax.sharding import PartitionSpec as P


count_cap = 100.0
power_law = 0.75
step_rate = 0.2

ROWS = 96
BLOCK = 120
HALF = 64
D = 300
LO = 256
MIB = 1 << 20


def pack_rows(main, tail):
    lane = lax.broadcasted_iota(jnp.int32, (24, 128), 1)
    low = lane < 64
    t = [tail[24 * g : 24 * g + 24, :] for g in range(4)]
    left = jnp.where(low, t[0], pltpu.roll(t[1], 64, 1))
    right = jnp.where(low, t[2], pltpu.roll(t[3], 64, 1))
    return jnp.concatenate([main, jnp.concatenate([left, right], axis=1)], axis=0)


def unpack_tail(packed):
    left, right = packed[ROWS:BLOCK, :128], packed[ROWS:BLOCK, 128:]
    return jnp.concatenate([left, pltpu.roll(left, 64, 1), right, pltpu.roll(right, 64, 1)], axis=0)


def to_column(row):
    eye = lax.broadcasted_iota(jnp.int32, (ROWS, ROWS), 0) == lax.broadcasted_iota(jnp.int32, (ROWS, ROWS), 1)
    return jnp.sum(jnp.where(eye, jnp.broadcast_to(row, (ROWS, ROWS)), 0.0), axis=1, keepdims=True)


def to_row(column):
    eye = lax.broadcasted_iota(jnp.int32, (ROWS, ROWS), 0) == lax.broadcasted_iota(jnp.int32, (ROWS, ROWS), 1)
    return jnp.sum(jnp.where(eye, jnp.broadcast_to(column, (ROWS, ROWS)), 0.0), axis=0, keepdims=True)


def pack_one(bias_lane, vec_ref, bias_ref, out_ref, tail_ref):
    tail_ref[...] = jnp.zeros_like(tail_ref)
    tail_ref[:, : D - LO] = vec_ref[:, LO:]
    lane = lax.broadcasted_iota(jnp.int32, (ROWS, 128), 1)
    tail = jnp.where(lane == bias_lane, jnp.broadcast_to(to_column(bias_ref[...]), (ROWS, 128)), tail_ref[...])
    out_ref[...] = pack_rows(vec_ref[:, :LO], tail).astype(jnp.bfloat16)


def pack_kernel(wv, wb, cv, cb, word_out, ctx_out, row_index, column_index, tail_ref):
    p, q = lax.axis_index("ctx"), lax.axis_index("word")
    y, z = lax.div(p, 4), lax.rem(p, 4)
    zl, x, c = lax.div(q, 8), lax.rem(lax.div(q, 2), 4), lax.rem(q, 2)
    for k in range(4):
        for j in range(4):
            row_index[4 * k + j] = lax.rem(y + k, 4) * 4 + lax.rem(z + j, 4)
    for i, (d, b, a) in enumerate((d, b, a) for d in (0, 1) for b in (0, 1, 3, 2) for a in (0, 1)):
        column_index[i] = lax.rem(zl + a, 2) * 8 + lax.rem(x + b, 4) * 2 + lax.rem(c + d, 2)
    pack_one(D - LO, wv, wb, word_out, tail_ref)
    pack_one(D - LO + 1, cv, cb, ctx_out, tail_ref)


def pack(word_vecs, word_bias, ctx_vecs, ctx_bias):
    return pl.pallas_call(
        pack_kernel,
        out_specs=[pl.BlockSpec(memory_space=pltpu.VMEM)] * 2 + [pl.BlockSpec(memory_space=pltpu.SMEM)] * 2,
        out_shape=[jax.ShapeDtypeStruct((BLOCK, LO), jnp.bfloat16)] * 2 + [jax.ShapeDtypeStruct((16,), jnp.int32)] * 2,
        scratch_shapes=[pltpu.VMEM((ROWS, 128), jnp.float32)],
        compiler_params=pltpu.CompilerParams(vmem_limit_bytes=4 * MIB),
        cost_estimate=pl.CostEstimate(flops=100000, bytes_accessed=400000, transcendentals=0),
        name="pack",
    )(*(pltpu.with_memory_space_constraint(v, pltpu.HBM) for v in (word_vecs, word_bias.reshape(1, ROWS), ctx_vecs, ctx_bias.reshape(1, ROWS))))


def weight_kernel(index_ref, counts_ref, weight_ref, log_ref):
    counts = counts_ref[...]
    values = counts.astype(jnp.float32)
    log_count = jnp.log(jnp.maximum(values, 1.0))
    power = jnp.exp(jnp.minimum(power_law * (log_count - jnp.log(jnp.float32(count_cap))), 0.0))
    weight_ref[...] = jnp.where(counts > 0, power, 0.0)
    log_ref[...] = log_count


def weights(k, index, counts):
    rows, columns = 4 * ROWS, counts.shape[1]
    spec = pl.BlockSpec((ROWS, columns), lambda j, index: (j, 0))
    return pl.pallas_call(
        weight_kernel,
        grid_spec=pltpu.PrefetchScalarGridSpec(
            num_scalar_prefetch=1,
            grid=(4,),
            in_specs=[pl.BlockSpec((ROWS, columns), lambda j, index: (index[4 * k + j], 0))],
            out_specs=[spec, spec],
        ),
        out_shape=[pltpu.VMEM((rows, columns), jnp.float32)] * 2,
        compiler_params=pltpu.CompilerParams(vmem_limit_bytes=6 * MIB),
        cost_estimate=pl.CostEstimate(
            flops=20 * rows * columns, bytes_accessed=12 * rows * columns, transcendentals=2 * rows * columns
        ),
    )(index, pltpu.with_memory_space_constraint(counts, pltpu.HBM))


def rows_of(index_ref, i):
    return pl.ds(pl.multiple_of(index_ref[i] * ROWS, ROWS), ROWS)


def word_chunk(blocks, weight, log_count, ctx_full, ctx_t, words, words_t, scaled_ref):
    lane = lax.broadcasted_iota(jnp.int32, (ROWS, 128), 1)
    bc = D - LO + 1
    for j in range(4):
        packed = blocks[j].astype(jnp.float32)
        tail = unpack_tail(packed)
        tail = jnp.where(lane < bc, tail, jnp.where(lane == bc, 1.0, 0.0))
        words[ROWS * j : ROWS * j + ROWS, :LO] = packed[:ROWS].astype(jnp.bfloat16)
        words[ROWS * j : ROWS * j + ROWS, LO:] = tail.astype(jnp.bfloat16)
    word_rows = words[...]
    words_t[...] = word_rows.T
    inner = jnp.dot(word_rows, ctx_t[...], preferred_element_type=jnp.float32)
    scaled_ref[...] = (weight[...] * (inner - log_count[...])).astype(jnp.bfloat16)
    term = jnp.dot(scaled_ref[...], ctx_full[...], preferred_element_type=jnp.float32)
    parts = [term[ROWS * j : ROWS * j + ROWS] for j in range(4)]
    return [pack_rows(part[:, :LO], part[:, LO:]) for part in parts]


def own_kernel(index_ref, w0, c0, c1, weight, log_count, grad, scaled, words_t, ctx_full, ctx_t, words):
    lane = lax.broadcasted_iota(jnp.int32, (ROWS, 128), 1)
    bw, bc = D - LO, D - LO + 1
    for i in range(16):
        packed = (c0 if i < 8 else c1)[i % 8].astype(jnp.float32)
        tail = unpack_tail(packed)
        tail = jnp.where(lane == bw, 1.0, jnp.where(lane <= bc, tail, 0.0))
        ctx_full[rows_of(index_ref, i), :LO] = packed[:ROWS].astype(jnp.bfloat16)
        ctx_full[rows_of(index_ref, i), LO:] = tail.astype(jnp.bfloat16)
    ctx_t[...] = ctx_full[...].T
    blocks = [w0[j] for j in range(4)]
    for j, packed in enumerate(word_chunk(blocks, weight, log_count, ctx_full, ctx_t, words, words_t, scaled)):
        grad[j] = packed


def near_kernel(w1, w3, k1, l1, k3, l3, ctx_full, ctx_t, g1, g3, scaled1, scaled3, words_t1, words_t3, words):
    for w, weight, log_count, grad, scaled, words_t in (
        (w1, k1, l1, g1, scaled1, words_t1), (w3, k3, l3, g3, scaled3, words_t3)
    ):
        blocks = [w[j] for j in range(4)]
        for j, packed in enumerate(word_chunk(blocks, weight, log_count, ctx_full, ctx_t, words, words_t, scaled)):
            grad[j] = packed.astype(jnp.bfloat16)


def far_kernel(w2a, w2b, weight, log_count, ctx_full, ctx_t, ga, gb, scaled, words_t, words):
    blocks = [(w2a, w2b)[j // 2][j % 2] for j in range(4)]
    for j, packed in enumerate(word_chunk(blocks, weight, log_count, ctx_full, ctx_t, words, words_t, scaled)):
        (ga, gb)[j // 2][j % 2] = packed.astype(jnp.bfloat16)


def ctx_kernel(index_ref, s0, s1, s2, s3, t0, t1, t2, t3, h_own, h_other, ctx_grad, back):
    for k, (t, s) in enumerate(((t0, s0), (t1, s1), (t2, s2), (t3, s3))):
        term = jnp.dot(t[...], s[...], preferred_element_type=jnp.float32)
        ctx_grad[...] = term if k == 0 else ctx_grad[...] + term
    back[...] = ctx_grad[...].T
    for i in range(16):
        term = back[rows_of(index_ref, i), :]
        packed = pack_rows(term[:, :LO], term[:, LO:])
        if i < 8:
            h_own[i] = packed
        else:
            h_other[i - 8] = packed.astype(jnp.bfloat16)


def sum_kernel(g0, rm, rp, ya, yb, own, nxt, last, far_a, far_b):
    f32 = jnp.float32
    for j, out in ((0, own), (1, nxt), (3, last), (2, None)):
        far = ya[j] if j < 2 else yb[j - 2]
        total = g0[j] + rm[j].astype(f32) + rp[j].astype(f32) + far.astype(f32)
        if out is None:
            far_a[...] = total[:HALF].astype(jnp.bfloat16)
            far_b[...] = total[HALF:].astype(jnp.bfloat16)
        else:
            out[...] = total


CHUNK, COLUMNS = 4 * ROWS, 16 * ROWS
SMEM_SPEC = pl.BlockSpec(memory_space=pltpu.SMEM)
VMEM_SPEC = pl.BlockSpec(memory_space=pltpu.VMEM)


def blocks_shape(n, dtype):
    return jax.ShapeDtypeStruct((n, BLOCK, LO), dtype)


def low_shape(*dims):
    return jax.ShapeDtypeStruct(dims, jnp.bfloat16)


def call(kernel, scalars, operands, out_shape, scratch, flops, limit):
    return pl.pallas_call(
        kernel,
        in_specs=[SMEM_SPEC] * len(scalars) + [VMEM_SPEC] * len(operands),
        out_specs=[VMEM_SPEC] * len(out_shape),
        out_shape=out_shape,
        scratch_shapes=scratch,
        compiler_params=pltpu.CompilerParams(vmem_limit_bytes=limit * MIB),
        cost_estimate=pl.CostEstimate(flops=flops, bytes_accessed=4 * MIB, transcendentals=0),
    )(*scalars, *operands)


CHUNK_FLOPS = 4 * CHUNK * COLUMNS * 384
WORDS_SCRATCH = [pltpu.VMEM((CHUNK, 384), jnp.bfloat16)]


def update_kernel(bias_lane, scale, total_ref, add_a, add_b, vec_ref, bias_ref, acc_ref, bacc_ref, nv, nb, na, nba):
    packed = total_ref[...] + add_a[...].astype(jnp.float32)
    if add_b is not None:
        packed = packed + add_b[...].astype(jnp.float32)
    packed = packed * scale
    tail = unpack_tail(packed)
    for columns, grad in ((slice(0, LO), packed[:ROWS]), (slice(LO, D), tail[:, : D - LO])):
        accum = acc_ref[:, columns] + grad * grad
        na[:, columns] = accum
        nv[:, columns] = vec_ref[:, columns] - step_rate * grad / jnp.sqrt(accum)
    grad = to_row(tail[:, bias_lane : bias_lane + 1])
    accum = bacc_ref[...] + grad * grad
    nba[...] = accum
    nb[...] = bias_ref[...] - step_rate * grad / jnp.sqrt(accum)


def update(total, add_a, add_b, vecs, bias, accum, bias_accum, bias_lane, scale):
    row = lambda a: a.reshape(1, ROWS)
    if add_b is None:
        kernel = lambda t, a, *rest: update_kernel(bias_lane, scale, t, a, None, *rest)
        sums = (total, add_a)
    else:
        kernel = functools.partial(update_kernel, bias_lane, scale)
        sums = (total, add_a, add_b)
    f32 = jnp.float32
    nv, nb, na, nba = pl.pallas_call(
        kernel,
        out_shape=[
            jax.ShapeDtypeStruct((ROWS, D), f32),
            jax.ShapeDtypeStruct((1, ROWS), f32),
            jax.ShapeDtypeStruct((ROWS, D), f32),
            jax.ShapeDtypeStruct((1, ROWS), f32),
        ],
        compiler_params=pltpu.CompilerParams(vmem_limit_bytes=6 * MIB),
        cost_estimate=pl.CostEstimate(flops=400000, bytes_accessed=800000, transcendentals=30000),
    )(*sums, vecs, row(bias), accum, row(bias_accum))
    return nv, nb.reshape(ROWS), na, nba.reshape(ROWS)


def ctx_shift(value, dy, dz):
    perm = [(i, ((i // 4 + dy) % 4) * 4 + (i % 4 + dz) % 4) for i in range(16)]
    return lax.ppermute(value, "ctx", perm)


def word_shift(value, dl, dx, dc):
    perm = [(i, ((i // 8 + dl) % 2) * 8 + ((i // 2 % 4 + dx) % 4) * 2 + (i % 2 + dc) % 2) for i in range(16)]
    return lax.ppermute(value, "word", perm)


def per_device(
    counts,
    word_vecs,
    word_bias,
    word_accum,
    word_bias_accum,
    ctx_vecs,
    ctx_bias,
    ctx_accum,
    ctx_bias_accum,
):
    f32, low = jnp.float32, jnp.bfloat16
    far_ctx = lambda v, dy, dz: ctx_shift(v, dy, dz)
    far_word = lambda v, dl, dx, dc: word_shift(v, dl, dx, dc)

    word_block, ctx_block, row_index, index = pack(word_vecs, word_bias, ctx_vecs, ctx_bias)

    zm, zp = far_ctx(word_block, 0, 1), far_ctx(word_block, 0, -1)
    pair = jnp.stack([ctx_block, far_word(ctx_block, 1, 0, 0)])
    xm, xp = far_word(pair, 0, 1, 0), far_word(pair, 0, -1, 0)
    zoa, zob = far_ctx(zm[:HALF], 0, 1), far_ctx(zp[HALF:], 0, -1)
    xoa, xob = far_word(xm[:1], 0, 1, 0), far_word(xp[1:], 0, -1, 0)
    w0 = jnp.stack([word_block, zp, jnp.concatenate([zoa, zob]), zm])
    w3, w1 = far_ctx(w0, 1, 0), far_ctx(w0, -1, 0)
    c0 = jnp.concatenate([pair, xp, xm, xoa, xob])
    c1 = far_word(c0, 0, 0, 1)
    w2a, w2b = far_ctx(w3[:2], 1, 0), far_ctx(w1[2:], -1, 0)

    weighted = []
    for k in range(4):
        pair_k = weights(k, row_index, counts)
        weighted.append([pltpu.with_memory_space_constraint(v, pltpu.VMEM) for v in pair_k])
    (k0, l0), (k1, l1), (k2, l2), (k3, l3) = weighted

    scaled_shape, words_t_shape = low_shape(CHUNK, COLUMNS), low_shape(384, CHUNK)
    g0, s0, t0, ctx_full, ctx_t = call(
        own_kernel, (index,), (w0, c0, c1, k0, l0),
        [blocks_shape(4, f32), scaled_shape, words_t_shape, low_shape(COLUMNS, 384), low_shape(384, COLUMNS)],
        WORDS_SCRATCH, CHUNK_FLOPS, 16,
    )
    g1, g3, s1, s3, t1, t3 = call(
        near_kernel, (), (w1, w3, k1, l1, k3, l3, ctx_full, ctx_t),
        [blocks_shape(4, low)] * 2 + [scaled_shape] * 2 + [words_t_shape] * 2,
        WORDS_SCRATCH, 2 * CHUNK_FLOPS, 16,
    )
    g2a, g2b, s2, t2 = call(
        far_kernel, (), (w2a, w2b, k2, l2, ctx_full, ctx_t),
        [blocks_shape(2, low)] * 2 + [scaled_shape, words_t_shape],
        WORDS_SCRATCH, CHUNK_FLOPS, 16,
    )
    h_own, h_other = call(
        ctx_kernel, (index,), (s0, s1, s2, s3, t0, t1, t2, t3),
        [blocks_shape(8, f32), blocks_shape(8, low)],
        [pltpu.VMEM((384, COLUMNS), f32), pltpu.VMEM((COLUMNS, 384), f32)], 2 * CHUNK_FLOPS, 16,
    )

    rm, rp = far_ctx(g1, 1, 0), far_ctx(g3, -1, 0)
    ya, yb = far_ctx(g2a, 1, 0), far_ctx(g2b, -1, 0)
    ya2, yb2 = far_ctx(ya, 1, 0), far_ctx(yb, -1, 0)
    hc = far_word(h_other, 0, 0, 1)
    s = h_own + hc.astype(f32)
    xa, xb = far_word(s[6:7].astype(low), 0, 1, 0), far_word(s[7:8].astype(low), 0, -1, 0)
    send_xp = jnp.concatenate([s[2:3] + xa.astype(f32), s[3:4]]).astype(low)
    send_xm = jnp.concatenate([s[4:5], s[5:6] + xb.astype(f32)]).astype(low)
    rxm, rxp = far_word(send_xp, 0, 1, 0), far_word(send_xm, 0, -1, 0)
    z_own, z_next, z_last, far_a, far_b = call(
        sum_kernel, (), (g0, rm, rp, ya2, yb2),
        [jax.ShapeDtypeStruct((BLOCK, LO), f32)] * 3 + [low_shape(HALF, LO), low_shape(BLOCK - HALF, LO)],
        [], 4 * BLOCK * LO * 4, 8,
    )
    za, zb = far_ctx(far_a, 0, 1), far_ctx(far_b, 0, -1)
    t = s[:2] + rxm.astype(f32) + rxp.astype(f32)
    rl = far_word(t[1].astype(low), 1, 0, 0)
    send_zp = jnp.concatenate([z_next[:HALF] + za.astype(f32), z_next[HALF:]]).astype(low)
    send_zm = jnp.concatenate([z_last[:HALF], z_last[HALF:] + zb.astype(f32)]).astype(low)
    rzm, rzp = far_ctx(send_zp, 0, 1), far_ctx(send_zm, 0, -1)

    word_scale = 2.0 / (counts.shape[1] * lax.axis_size("ctx"))
    ctx_scale = 2.0 / (counts.shape[0] * lax.axis_size("word"))
    new_ctx_vecs, new_ctx_bias, new_ctx_accum, new_ctx_bias_accum = update(
        t[0], rl, None, ctx_vecs, ctx_bias, ctx_accum, ctx_bias_accum, D - LO + 1, ctx_scale
    )
    new_word_vecs, new_word_bias, new_word_accum, new_word_bias_accum = update(
        z_own, rzm, rzp, word_vecs, word_bias, word_accum, word_bias_accum, D - LO, word_scale
    )
    return (
        new_word_vecs,
        new_word_bias,
        new_word_accum,
        new_word_bias_accum,
        new_ctx_vecs,
        new_ctx_bias,
        new_ctx_accum,
        new_ctx_bias_accum,
    )


def solution(mesh):
    words, contexts = P(("word", "ctx")), P(("ctx", "word"))
    return jax.shard_map(
        per_device,
        mesh=mesh,
        in_specs=(P("word", "ctx"), words, words, words, words, contexts, contexts, contexts, contexts),
        out_specs=(words, words, words, words, contexts, contexts, contexts, contexts),
        check_vma=False,
    )
```

```python
import functools
import math

import jax
import jax.numpy as jnp
from jax import lax
from jax.experimental import pallas as pl
from jax.experimental.pallas import tpu as pltpu
from jax.sharding import PartitionSpec as P


count_cap = 100.0
power_law = 0.75
step_rate = 0.2

ROWS = 96
BLOCK = 120
D = 300
LO = 256
MIB = 1 << 20


def pack_rows(main, tail):
    lane = lax.broadcasted_iota(jnp.int32, (24, 128), 1)
    low = lane < 64
    t = [tail[24 * g : 24 * g + 24, :] for g in range(4)]
    left = jnp.where(low, t[0], pltpu.roll(t[1], 64, 1))
    right = jnp.where(low, t[2], pltpu.roll(t[3], 64, 1))
    return jnp.concatenate([main, jnp.concatenate([left, right], axis=1)], axis=0)


def unpack_tail(packed):
    left, right = packed[ROWS:BLOCK, :128], packed[ROWS:BLOCK, 128:]
    return jnp.concatenate([left, pltpu.roll(left, 64, 1), right, pltpu.roll(right, 64, 1)], axis=0)


def to_column(row):
    eye = lax.broadcasted_iota(jnp.int32, (ROWS, ROWS), 0) == lax.broadcasted_iota(jnp.int32, (ROWS, ROWS), 1)
    return jnp.sum(jnp.where(eye, jnp.broadcast_to(row, (ROWS, ROWS)), 0.0), axis=1, keepdims=True)


def to_row(column):
    eye = lax.broadcasted_iota(jnp.int32, (ROWS, ROWS), 0) == lax.broadcasted_iota(jnp.int32, (ROWS, ROWS), 1)
    return jnp.sum(jnp.where(eye, jnp.broadcast_to(column, (ROWS, ROWS)), 0.0), axis=0, keepdims=True)


def pack_one(bias_lane, vec_ref, bias_ref, out_ref, tail_ref):
    tail_ref[...] = jnp.zeros_like(tail_ref)
    tail_ref[:, : D - LO] = vec_ref[:, LO:]
    lane = lax.broadcasted_iota(jnp.int32, (ROWS, 128), 1)
    tail = jnp.where(lane == bias_lane, jnp.broadcast_to(to_column(bias_ref[...]), (ROWS, 128)), tail_ref[...])
    out_ref[...] = pack_rows(vec_ref[:, :LO], tail).astype(jnp.bfloat16)


PIECES = (
    (0, 0, 0), (0, 0, 1), (1, 0, 0), (1, 0, 1), (0, -1, 0), (0, -1, 1), (1, -1, 0), (1, -1, 1), (0, 2, 0), (0, 2, 1),
    (1, 1, 0), (1, 1, 1), (0, 1, 0), (0, 1, 1), (1, 2, 0), (1, 2, 1),
)
RESULTS = tuple((d, b if d == 0 else -b, a) for d in (0, 1) for b in range(4) for a in (0, 1))


def pack_kernel(wv, wb, cv, cb, word_out, ctx_out, row_index, piece_index, result_index, tail_ref):
    p, q = lax.axis_index("ctx"), lax.axis_index("word")
    y, z = lax.div(p, 4), lax.rem(p, 4)
    zl, x, c = lax.div(q, 8), lax.rem(lax.div(q, 2), 4), lax.rem(q, 2)
    s = 1 - 2 * c
    for k in range(4):
        for j in range(4):
            row_index[4 * k + j] = lax.rem(y + k * s + 4, 4) * 4 + lax.rem(z + j * s + 4, 4)
    for out, table in ((piece_index, PIECES), (result_index, RESULTS)):
        for i, (d, b, a) in enumerate(table):
            out[i] = lax.rem(zl + a, 2) * 8 + lax.rem(x + b * s + 4, 4) * 2 + lax.rem(c + d, 2)
    pack_one(D - LO, wv, wb, word_out, tail_ref)
    pack_one(D - LO + 1, cv, cb, ctx_out, tail_ref)


def pack(word_vecs, word_bias, ctx_vecs, ctx_bias):
    return pl.pallas_call(
        pack_kernel,
        out_specs=[pl.BlockSpec(memory_space=pltpu.VMEM)] * 2 + [pl.BlockSpec(memory_space=pltpu.SMEM)] * 3,
        out_shape=[jax.ShapeDtypeStruct((BLOCK, LO), jnp.bfloat16)] * 2 + [jax.ShapeDtypeStruct((16,), jnp.int32)] * 3,
        scratch_shapes=[pltpu.VMEM((ROWS, 128), jnp.float32)],
        compiler_params=pltpu.CompilerParams(vmem_limit_bytes=4 * MIB),
        cost_estimate=pl.CostEstimate(flops=100000, bytes_accessed=400000, transcendentals=0),
        name="pack",
    )(*(pltpu.with_memory_space_constraint(v, pltpu.HBM) for v in (word_vecs, word_bias.reshape(1, ROWS), ctx_vecs, ctx_bias.reshape(1, ROWS))))


def weight_kernel(chunks, index_ref, counts, *refs):
    outs, (held, sems) = refs[:-2], refs[-2:]

    def fetch(n):
        start = pl.multiple_of(index_ref[4 * chunks[n // 4] + n % 4] * ROWS, ROWS)
        return pltpu.make_async_copy(counts.at[pl.ds(start, ROWS)], held.at[n], sems.at[n])

    copies = [fetch(n) for n in range(4 * len(chunks))]
    for copy in copies:
        copy.start()
    for n, copy in enumerate(copies):
        weight_ref, log_ref = outs[n // 4 * 2], outs[n // 4 * 2 + 1]
        copy.wait()

        def step(i, _):
            rows = pl.ds(pl.multiple_of(i * 8, 8), 8)
            count = held[n, rows, :]
            log_count = jnp.log(jnp.maximum(count, 1).astype(jnp.float32))
            power = jnp.exp(jnp.minimum(power_law * (log_count - math.log(count_cap)), 0.0))
            to = pl.ds(pl.multiple_of(n % 4 * ROWS + i * 8, 8), 8)
            weight_ref[to, :] = jnp.where(count > 0, power, 0.0)
            log_ref[to, :] = log_count
            return 0

        lax.fori_loop(0, ROWS // 8, step, 0, unroll=3)


def weights(chunks, index, counts):
    columns, n = counts.shape[1], len(chunks)
    return pl.pallas_call(
        functools.partial(weight_kernel, chunks),
        in_specs=[pl.BlockSpec(memory_space=pltpu.SMEM), pl.BlockSpec(memory_space=pltpu.HBM)],
        out_specs=[pl.BlockSpec(memory_space=pltpu.VMEM)] * (2 * n),
        out_shape=[pltpu.VMEM((4 * ROWS, columns), jnp.float32)] * (2 * n),
        scratch_shapes=[pltpu.VMEM((4 * n, ROWS, columns), jnp.int32), pltpu.SemaphoreType.DMA((4 * n,))],
        compiler_params=pltpu.CompilerParams(vmem_limit_bytes=8 * MIB),
        cost_estimate=pl.CostEstimate(
            flops=80 * n * ROWS * columns, bytes_accessed=48 * n * ROWS * columns, transcendentals=8 * n * ROWS * columns
        ),
    )(index, pltpu.with_memory_space_constraint(counts, pltpu.HBM))


def rows_of(index_ref, i):
    return pl.ds(pl.multiple_of(index_ref[i] * ROWS, ROWS), ROWS)


def word_chunk(blocks, weight, log_count, ctx_full, ctx_t, words, words_t, scaled_ref):
    lane = lax.broadcasted_iota(jnp.int32, (ROWS, 128), 1)
    bc = D - LO + 1
    for j in range(4):
        packed = blocks[j].astype(jnp.float32)
        tail = unpack_tail(packed)
        tail = jnp.where(lane < bc, tail, jnp.where(lane == bc, 1.0, 0.0))
        words[ROWS * j : ROWS * j + ROWS, :LO] = packed[:ROWS].astype(jnp.bfloat16)
        words[ROWS * j : ROWS * j + ROWS, LO:] = tail.astype(jnp.bfloat16)
    word_rows = words[...]
    words_t[...] = word_rows.T
    inner = jnp.dot(word_rows, ctx_t[...], preferred_element_type=jnp.float32)
    scaled_ref[...] = (weight[...] * (inner - log_count[...])).astype(jnp.bfloat16)
    term = jnp.dot(scaled_ref[...], ctx_full[...], preferred_element_type=jnp.float32)
    parts = [term[ROWS * j : ROWS * j + ROWS] for j in range(4)]
    return [pack_rows(part[:, :LO], part[:, LO:]) for part in parts]


def own_kernel(index_ref, w0, c0, c1, weight, log_count, grad, scaled, words_t, ctx_full, ctx_t, words):
    lane = lax.broadcasted_iota(jnp.int32, (ROWS, 128), 1)
    bw, bc = D - LO, D - LO + 1
    for i in range(16):
        packed = (c0[i] if i < 10 else c1[i - 10]).astype(jnp.float32)
        tail = unpack_tail(packed)
        tail = jnp.where(lane == bw, 1.0, jnp.where(lane <= bc, tail, 0.0))
        ctx_full[rows_of(index_ref, i), :LO] = packed[:ROWS].astype(jnp.bfloat16)
        ctx_full[rows_of(index_ref, i), LO:] = tail.astype(jnp.bfloat16)
    ctx_t[...] = ctx_full[...].T
    blocks = [w0[j] for j in range(4)]
    for j, packed in enumerate(word_chunk(blocks, weight, log_count, ctx_full, ctx_t, words, words_t, scaled)):
        grad[j] = packed


def near_kernel(w1, w3, k1, l1, k3, l3, ctx_full, ctx_t, g1, g3, scaled1, scaled3, words_t1, words_t3, words):
    for w, weight, log_count, grad, scaled, words_t in (
        (w1, k1, l1, g1, scaled1, words_t1), (w3, k3, l3, g3, scaled3, words_t3)
    ):
        blocks = [w[j] for j in range(4)]
        for j, packed in enumerate(word_chunk(blocks, weight, log_count, ctx_full, ctx_t, words, words_t, scaled)):
            grad[j] = packed.astype(jnp.bfloat16)


def far_kernel(w2, weight, log_count, ctx_full, ctx_t, grad, scaled, words_t, words):
    blocks = [w2[j] for j in range(4)]
    for j, packed in enumerate(word_chunk(blocks, weight, log_count, ctx_full, ctx_t, words, words_t, scaled)):
        grad[j] = packed.astype(jnp.bfloat16)


def ctx_kernel(index_ref, s0, s1, s2, s3, t0, t1, t2, t3, h_own, h_other, ctx_grad, back):
    for k, (t, s) in enumerate(((t0, s0), (t1, s1), (t2, s2), (t3, s3))):
        term = jnp.dot(t[...], s[...], preferred_element_type=jnp.float32)
        ctx_grad[...] = term if k == 0 else ctx_grad[...] + term
    back[...] = ctx_grad[...].T
    for i in range(16):
        term = back[rows_of(index_ref, i), :]
        packed = pack_rows(term[:, :LO], term[:, LO:])
        if i < 8:
            h_own[i] = packed
        else:
            h_other[i - 8] = packed.astype(jnp.bfloat16)


def sum_kernel(g0, rn, f2, ya, own, nxt, far, back):
    f32 = jnp.float32
    for j, out in enumerate((own, nxt, far, back)):
        total = g0[j] + rn[j].astype(f32) + f2[j].astype(f32) + ya[j].astype(f32)
        out[...] = total.astype(out.dtype)


CHUNK, COLUMNS = 4 * ROWS, 16 * ROWS
SMEM_SPEC = pl.BlockSpec(memory_space=pltpu.SMEM)
VMEM_SPEC = pl.BlockSpec(memory_space=pltpu.VMEM)


def blocks_shape(n, dtype):
    return jax.ShapeDtypeStruct((n, BLOCK, LO), dtype)


def low_shape(*dims):
    return jax.ShapeDtypeStruct(dims, jnp.bfloat16)


def call(kernel, scalars, operands, out_shape, scratch, flops, limit):
    return pl.pallas_call(
        kernel,
        in_specs=[SMEM_SPEC] * len(scalars) + [VMEM_SPEC] * len(operands),
        out_specs=[VMEM_SPEC] * len(out_shape),
        out_shape=out_shape,
        scratch_shapes=scratch,
        compiler_params=pltpu.CompilerParams(vmem_limit_bytes=limit * MIB),
        cost_estimate=pl.CostEstimate(flops=flops, bytes_accessed=4 * MIB, transcendentals=0),
    )(*scalars, *operands)


CHUNK_FLOPS = 4 * CHUNK * COLUMNS * 384
WORDS_SCRATCH = [pltpu.VMEM((CHUNK, 384), jnp.bfloat16)]


def update_kernel(bias_lane, scale, total_ref, add_a, add_b, vec_ref, bias_ref, acc_ref, bacc_ref, nv, nb, na, nba):
    packed = total_ref[...] + (add_a[0] if len(add_a.shape) == 3 else add_a[...]).astype(jnp.float32)
    if add_b is not None:
        packed = packed + add_b[...].astype(jnp.float32)
    packed = packed * scale
    tail = unpack_tail(packed)
    for columns, grad in ((slice(0, LO), packed[:ROWS]), (slice(LO, D), tail[:, : D - LO])):
        accum = acc_ref[:, columns] + grad * grad
        na[:, columns] = accum
        nv[:, columns] = vec_ref[:, columns] - step_rate * grad / jnp.sqrt(accum)
    grad = to_row(tail[:, bias_lane : bias_lane + 1])
    accum = bacc_ref[...] + grad * grad
    nba[...] = accum
    nb[...] = bias_ref[...] - step_rate * grad / jnp.sqrt(accum)


def update(total, add_a, add_b, vecs, bias, accum, bias_accum, bias_lane, scale):
    row = lambda a: a.reshape(1, ROWS)
    if add_b is None:
        kernel = lambda t, a, *rest: update_kernel(bias_lane, scale, t, a, None, *rest)
        sums = (total, add_a)
    else:
        kernel = functools.partial(update_kernel, bias_lane, scale)
        sums = (total, add_a, add_b)
    f32 = jnp.float32
    nv, nb, na, nba = pl.pallas_call(
        kernel,
        out_shape=[
            jax.ShapeDtypeStruct((ROWS, D), f32),
            jax.ShapeDtypeStruct((1, ROWS), f32),
            jax.ShapeDtypeStruct((ROWS, D), f32),
            jax.ShapeDtypeStruct((1, ROWS), f32),
        ],
        compiler_params=pltpu.CompilerParams(vmem_limit_bytes=6 * MIB),
        cost_estimate=pl.CostEstimate(flops=400000, bytes_accessed=800000, transcendentals=30000),
    )(*sums, vecs, row(bias), accum, row(bias_accum))
    return nv, nb.reshape(ROWS), na, nba.reshape(ROWS)


def spread(index):
    q, p = index // 16, index % 16
    return q // 8, q // 2 % 4, q % 2, p // 4, p % 4


def place(zl, x, c, y, z):
    return (zl % 2 * 8 + x % 4 * 2 + c % 2) * 16 + y % 4 * 4 + z % 4


def move(value, axis):
    perm = []
    for i in range(256):
        zl, x, c, y, z = spread(i)
        s = 1 - 2 * c
        to = {
            "core": (zl, x, c + 1, y, z),
            "zl": (zl + 1, x, c, y, z),
            "x": (zl, x + s, c, y, z),
            "y": (zl, x, c, y + s, z),
            "z": (zl, x, c, y, z + s),
        }[axis]
        perm.append((i, place(*to)))
    return lax.ppermute(value, ("word", "ctx"), perm)


def keep(arrays):
    return [pltpu.with_memory_space_constraint(v, pltpu.VMEM) for v in arrays]


def per_device(
    counts,
    word_vecs,
    word_bias,
    word_accum,
    word_bias_accum,
    ctx_vecs,
    ctx_bias,
    ctx_accum,
    ctx_bias_accum,
):
    f32, low = jnp.float32, jnp.bfloat16
    go = lambda value, axis: move(value, axis)

    word_block, ctx_block, row_index, piece_index, result_index = pack(word_vecs, word_bias, ctx_vecs, ctx_bias)

    both = jnp.stack([word_block, go(word_block, "core")])
    pair = jnp.stack([ctx_block, go(ctx_block, "zl")])
    zr1 = go(both, "z")
    four = jnp.concatenate([pair, go(pair, "core")])
    zr2 = go(zr1[:1], "z")
    xr1 = go(four, "x")
    e1 = go(jnp.concatenate([zr1[1:], zr1[:1], zr2]), "core")
    wy = jnp.concatenate([both[:1], e1[:1], zr2, zr1[:1], both[1:], zr1[1:], e1[2:], e1[1:2]])
    yr1 = go(wy, "y")
    xr2 = go(xr1[:2], "x")
    c0 = jnp.concatenate([four, xr1, xr2])
    c1 = go(c0[4:], "core")
    w2 = go(yr1[:4], "y")
    w1 = go(yr1[4:], "core")

    k0, l0, k1, l1 = keep(weights((0, 1), row_index, counts))
    k3, l3, k2, l2 = keep(weights((3, 2), row_index, counts))
    scaled_shape, words_t_shape = low_shape(CHUNK, COLUMNS), low_shape(384, CHUNK)
    g0, s0, t0, ctx_full, ctx_t = call(
        own_kernel, (piece_index,), (wy, c0, c1, k0, l0),
        [blocks_shape(4, f32), scaled_shape, words_t_shape, low_shape(COLUMNS, 384), low_shape(384, COLUMNS)],
        WORDS_SCRATCH, CHUNK_FLOPS, 16,
    )
    g1, g3, s1, s3, t1, t3 = call(
        near_kernel, (), (w1, yr1, k1, l1, k3, l3, ctx_full, ctx_t),
        [blocks_shape(4, low)] * 2 + [scaled_shape] * 2 + [words_t_shape] * 2,
        WORDS_SCRATCH, 2 * CHUNK_FLOPS, 16,
    )
    g2, s2, t2 = call(
        far_kernel, (), (w2, k2, l2, ctx_full, ctx_t),
        [blocks_shape(4, low), scaled_shape, words_t_shape],
        WORDS_SCRATCH, CHUNK_FLOPS, 16,
    )
    h_own, h_other = call(
        ctx_kernel, (result_index,), (s0, s1, s2, s3, t0, t1, t2, t3),
        [blocks_shape(8, f32), blocks_shape(8, low)],
        [pltpu.VMEM((384, COLUMNS), f32), pltpu.VMEM((COLUMNS, 384), f32)], 2 * CHUNK_FLOPS, 16,
    )

    f1 = go(g3, "core")
    ya = go(g2, "y")
    rn = go(jnp.concatenate([g1, f1]), "y")
    hc = go(h_other, "core")
    ya2 = go(ya, "y")
    s = h_own + hc.astype(f32)
    xa, x3 = go(s[4:6].astype(low), "x"), go(s[6:8].astype(low), "core")
    f2 = go(rn[4:], "core")
    z_own, z_next, z_far, z_back = call(
        sum_kernel, (), (g0, rn, f2, ya2),
        [jax.ShapeDtypeStruct((BLOCK, LO), f32)] * 2 + [low_shape(BLOCK, LO)] * 2, [], 4 * BLOCK * LO * 4, 8,
    )
    za, f3 = go(z_far, "z"), go(z_back, "core")
    xr = go(jnp.concatenate([(s[2:4] + xa.astype(f32)).astype(low), x3]), "x")
    x4 = go(xr[2:], "core")
    rz = go(jnp.stack([(z_next + za.astype(f32)).astype(low), f3]), "z")
    t = s[:2] + xr[:2].astype(f32) + x4.astype(f32)
    rl = go(t[1].astype(low), "zl")
    f4 = go(rz[1], "core")

    word_scale = 2.0 / (counts.shape[1] * lax.axis_size("ctx"))
    ctx_scale = 2.0 / (counts.shape[0] * lax.axis_size("word"))
    new_ctx_vecs, new_ctx_bias, new_ctx_accum, new_ctx_bias_accum = update(
        t[0], rl, None, ctx_vecs, ctx_bias, ctx_accum, ctx_bias_accum, D - LO + 1, ctx_scale
    )
    new_word_vecs, new_word_bias, new_word_accum, new_word_bias_accum = update(
        z_own, rz, f4, word_vecs, word_bias, word_accum, word_bias_accum, D - LO, word_scale
    )
    return (
        new_word_vecs,
        new_word_bias,
        new_word_accum,
        new_word_bias_accum,
        new_ctx_vecs,
        new_ctx_bias,
        new_ctx_accum,
        new_ctx_bias_accum,
    )


def solution(mesh):
    words, contexts = P(("word", "ctx")), P(("ctx", "word"))
    return jax.shard_map(
        per_device,
        mesh=mesh,
        in_specs=(P("word", "ctx"), words, words, words, words, contexts, contexts, contexts, contexts),
        out_specs=(words, words, words, words, contexts, contexts, contexts, contexts),
        check_vma=False,
    )
```

```python
import functools
import math

import jax
import jax.numpy as jnp
from jax import lax
from jax.experimental import pallas as pl
from jax.experimental.pallas import tpu as pltpu
from jax.sharding import PartitionSpec as P


count_cap = 100.0
power_law = 0.75
step_rate = 0.2

ROWS = 96
BLOCK = 120
D = 300
LO = 256
MIB = 1 << 20


def pack_rows(main, tail):
    lane = lax.broadcasted_iota(jnp.int32, (24, 128), 1)
    low = lane < 64
    t = [tail[24 * g : 24 * g + 24, :] for g in range(4)]
    left = jnp.where(low, t[0], pltpu.roll(t[1], 64, 1))
    right = jnp.where(low, t[2], pltpu.roll(t[3], 64, 1))
    return jnp.concatenate([main, jnp.concatenate([left, right], axis=1)], axis=0)


def unpack_tail(packed):
    left, right = packed[ROWS:BLOCK, :128], packed[ROWS:BLOCK, 128:]
    return jnp.concatenate([left, pltpu.roll(left, 64, 1), right, pltpu.roll(right, 64, 1)], axis=0)


def to_column(row):
    eye = lax.broadcasted_iota(jnp.int32, (ROWS, ROWS), 0) == lax.broadcasted_iota(jnp.int32, (ROWS, ROWS), 1)
    return jnp.sum(jnp.where(eye, jnp.broadcast_to(row, (ROWS, ROWS)), 0.0), axis=1, keepdims=True)


def to_row(column):
    eye = lax.broadcasted_iota(jnp.int32, (ROWS, ROWS), 0) == lax.broadcasted_iota(jnp.int32, (ROWS, ROWS), 1)
    return jnp.sum(jnp.where(eye, jnp.broadcast_to(column, (ROWS, ROWS)), 0.0), axis=0, keepdims=True)


def pack_one(bias_lane, vec_ref, bias_ref, out_ref, tail_ref):
    tail_ref[...] = jnp.zeros_like(tail_ref)
    tail_ref[:, : D - LO] = vec_ref[:, LO:]
    lane = lax.broadcasted_iota(jnp.int32, (ROWS, 128), 1)
    tail = jnp.where(lane == bias_lane, jnp.broadcast_to(to_column(bias_ref[...]), (ROWS, 128)), tail_ref[...])
    out_ref[...] = pack_rows(vec_ref[:, :LO], tail).astype(jnp.bfloat16)


PIECES = (
    (0, 0, 0), (0, 0, 1), (1, 0, 0), (1, 0, 1), (0, -1, 0), (0, -1, 1), (1, -1, 0), (1, -1, 1), (0, 2, 0), (0, 2, 1),
    (1, 1, 0), (1, 1, 1), (0, 1, 0), (0, 1, 1), (1, 2, 0), (1, 2, 1),
)
RESULTS = tuple((d, b if d == 0 else -b, a) for d in (0, 1) for b in range(4) for a in (0, 1))


def pack_kernel(wv, wb, cv, cb, word_out, ctx_out, row_index, piece_index, result_index, tail_ref):
    p, q = lax.axis_index("ctx"), lax.axis_index("word")
    y, z = lax.div(p, 4), lax.rem(p, 4)
    zl, x, c = lax.div(q, 8), lax.rem(lax.div(q, 2), 4), lax.rem(q, 2)
    s = 1 - 2 * c
    for k in range(4):
        for j in range(4):
            row_index[4 * k + j] = lax.rem(y + k * s + 4, 4) * 4 + lax.rem(z + j * s + 4, 4)
    for out, table in ((piece_index, PIECES), (result_index, RESULTS)):
        for i, (d, b, a) in enumerate(table):
            out[i] = lax.rem(zl + a, 2) * 8 + lax.rem(x + b * s + 4, 4) * 2 + lax.rem(c + d, 2)
    pack_one(D - LO, wv, wb, word_out, tail_ref)
    pack_one(D - LO + 1, cv, cb, ctx_out, tail_ref)


def pack(word_vecs, word_bias, ctx_vecs, ctx_bias):
    return pl.pallas_call(
        pack_kernel,
        out_specs=[pl.BlockSpec(memory_space=pltpu.VMEM)] * 2 + [pl.BlockSpec(memory_space=pltpu.SMEM)] * 3,
        out_shape=[jax.ShapeDtypeStruct((BLOCK, LO), jnp.bfloat16)] * 2 + [jax.ShapeDtypeStruct((16,), jnp.int32)] * 3,
        scratch_shapes=[pltpu.VMEM((ROWS, 128), jnp.float32)],
        compiler_params=pltpu.CompilerParams(vmem_limit_bytes=4 * MIB),
        cost_estimate=pl.CostEstimate(flops=100000, bytes_accessed=400000, transcendentals=0),
        name="pack",
    )(*(pltpu.with_memory_space_constraint(v, pltpu.HBM) for v in (word_vecs, word_bias.reshape(1, ROWS), ctx_vecs, ctx_bias.reshape(1, ROWS))))


def weight_kernel(chunks, index_ref, counts, *refs):
    outs, (held, sems) = refs[:-2], refs[-2:]

    def fetch(n):
        start = pl.multiple_of(index_ref[4 * chunks[n // 4] + n % 4] * ROWS, ROWS)
        return pltpu.make_async_copy(counts.at[pl.ds(start, ROWS)], held.at[n], sems.at[n])

    copies = [fetch(n) for n in range(4 * len(chunks))]
    for copy in copies:
        copy.start()
    for n, copy in enumerate(copies):
        weight_ref, log_ref = outs[n // 4 * 2], outs[n // 4 * 2 + 1]
        copy.wait()

        def step(i, _):
            rows = pl.ds(pl.multiple_of(i * 8, 8), 8)
            count = held[n, rows, :]
            log_count = jnp.log(jnp.maximum(count, 1).astype(jnp.float32))
            power = jnp.exp(jnp.minimum(power_law * (log_count - math.log(count_cap)), 0.0))
            to = pl.ds(pl.multiple_of(n % 4 * ROWS + i * 8, 8), 8)
            weight_ref[to, :] = jnp.where(count > 0, power, 0.0)
            log_ref[to, :] = log_count
            return 0

        lax.fori_loop(0, ROWS // 8, step, 0, unroll=3)


def weights(chunks, index, counts):
    columns, n = counts.shape[1], len(chunks)
    return pl.pallas_call(
        functools.partial(weight_kernel, chunks),
        in_specs=[pl.BlockSpec(memory_space=pltpu.SMEM), pl.BlockSpec(memory_space=pltpu.HBM)],
        out_specs=[pl.BlockSpec(memory_space=pltpu.VMEM)] * (2 * n),
        out_shape=[pltpu.VMEM((4 * ROWS, columns), jnp.float32)] * (2 * n),
        scratch_shapes=[pltpu.VMEM((4 * n, ROWS, columns), jnp.int32), pltpu.SemaphoreType.DMA((4 * n,))],
        compiler_params=pltpu.CompilerParams(vmem_limit_bytes=8 * MIB),
        cost_estimate=pl.CostEstimate(
            flops=80 * n * ROWS * columns, bytes_accessed=48 * n * ROWS * columns, transcendentals=8 * n * ROWS * columns
        ),
    )(index, pltpu.with_memory_space_constraint(counts, pltpu.HBM))


def rows_of(index_ref, i):
    return pl.ds(pl.multiple_of(index_ref[i] * ROWS, ROWS), ROWS)


def word_chunk(blocks, weight, log_count, ctx_full, ctx_t, words, words_t, scaled_ref):
    lane = lax.broadcasted_iota(jnp.int32, (ROWS, 128), 1)
    bc = D - LO + 1
    for j in range(4):
        packed = blocks[j].astype(jnp.float32)
        tail = unpack_tail(packed)
        tail = jnp.where(lane < bc, tail, jnp.where(lane == bc, 1.0, 0.0))
        words[ROWS * j : ROWS * j + ROWS, :LO] = packed[:ROWS].astype(jnp.bfloat16)
        words[ROWS * j : ROWS * j + ROWS, LO:] = tail.astype(jnp.bfloat16)
    word_rows = words[...]
    words_t[...] = word_rows.T
    inner = jnp.dot(word_rows, ctx_t[...], preferred_element_type=jnp.float32)
    scaled_ref[...] = (weight[...] * (inner - log_count[...])).astype(jnp.bfloat16)
    term = jnp.dot(scaled_ref[...], ctx_full[...], preferred_element_type=jnp.float32)
    parts = [term[ROWS * j : ROWS * j + ROWS] for j in range(4)]
    return [pack_rows(part[:, :LO], part[:, LO:]) for part in parts]


def build(index_ref, c0, c1, ctx_full, ctx_t):
    lane = lax.broadcasted_iota(jnp.int32, (ROWS, 128), 1)
    bw, bc = D - LO, D - LO + 1
    for i in range(16):
        packed = (c0[i] if i < 10 else c1[i - 10]).astype(jnp.float32)
        tail = unpack_tail(packed)
        tail = jnp.where(lane == bw, 1.0, jnp.where(lane <= bc, tail, 0.0))
        ctx_full[rows_of(index_ref, i), :LO] = packed[:ROWS].astype(jnp.bfloat16)
        ctx_full[rows_of(index_ref, i), LO:] = tail.astype(jnp.bfloat16)
    ctx_t[...] = ctx_full[...].T


def chunk_kernel(w, weight, log_count, ctx_full, ctx_t, grad, scaled, words_t, words):
    blocks = [w[j] for j in range(4)]
    for j, packed in enumerate(word_chunk(blocks, weight, log_count, ctx_full, ctx_t, words, words_t, scaled)):
        grad[j] = packed.astype(grad.dtype)


def first_kernel(index_ref, w, c0, c1, weight, log_count, grad, scaled, words_t, ctx_full, ctx_t, words):
    build(index_ref, c0, c1, ctx_full, ctx_t)
    chunk_kernel(w, weight, log_count, ctx_full, ctx_t, grad, scaled, words_t, words)


def ctx_kernel(index_ref, s0, s1, s2, s3, t0, t1, t2, t3, h_own, h_other, ctx_grad, back):
    for k, (t, s) in enumerate(((t0, s0), (t1, s1), (t2, s2), (t3, s3))):
        term = jnp.dot(t[...], s[...], preferred_element_type=jnp.float32)
        ctx_grad[...] = term if k == 0 else ctx_grad[...] + term
    back[...] = ctx_grad[...].T
    for i in range(16):
        term = back[rows_of(index_ref, i), :]
        packed = pack_rows(term[:, :LO], term[:, LO:])
        if i < 8:
            h_own[i] = packed
        else:
            h_other[i - 8] = packed.astype(jnp.bfloat16)


def sum_kernel(g0, rn, f2, ya, own, nxt, far, back):
    f32 = jnp.float32
    for j, out in enumerate((own, nxt, far, back)):
        total = g0[j] + rn[j].astype(f32) + f2[j].astype(f32) + ya[j].astype(f32)
        out[...] = total.astype(out.dtype)


CHUNK, COLUMNS = 4 * ROWS, 16 * ROWS
SMEM_SPEC = pl.BlockSpec(memory_space=pltpu.SMEM)
VMEM_SPEC = pl.BlockSpec(memory_space=pltpu.VMEM)


def blocks_shape(n, dtype):
    return jax.ShapeDtypeStruct((n, BLOCK, LO), dtype)


def low_shape(*dims):
    return jax.ShapeDtypeStruct(dims, jnp.bfloat16)


def call(kernel, scalars, operands, out_shape, scratch, flops, limit):
    return pl.pallas_call(
        kernel,
        in_specs=[SMEM_SPEC] * len(scalars) + [VMEM_SPEC] * len(operands),
        out_specs=[VMEM_SPEC] * len(out_shape),
        out_shape=out_shape,
        scratch_shapes=scratch,
        compiler_params=pltpu.CompilerParams(vmem_limit_bytes=limit * MIB),
        cost_estimate=pl.CostEstimate(flops=flops, bytes_accessed=4 * MIB, transcendentals=0),
    )(*scalars, *operands)


CHUNK_FLOPS = 4 * CHUNK * COLUMNS * 384
WORDS_SCRATCH = [pltpu.VMEM((CHUNK, 384), jnp.bfloat16)]


def update_kernel(bias_lane, scale, total_ref, add_a, add_b, vec_ref, bias_ref, acc_ref, bacc_ref, nv, nb, na, nba):
    packed = total_ref[...] + (add_a[0] if len(add_a.shape) == 3 else add_a[...]).astype(jnp.float32)
    if add_b is not None:
        packed = packed + add_b[...].astype(jnp.float32)
    packed = packed * scale
    tail = unpack_tail(packed)
    for columns, grad in ((slice(0, LO), packed[:ROWS]), (slice(LO, D), tail[:, : D - LO])):
        accum = acc_ref[:, columns] + grad * grad
        na[:, columns] = accum
        nv[:, columns] = vec_ref[:, columns] - step_rate * grad / jnp.sqrt(accum)
    grad = to_row(tail[:, bias_lane : bias_lane + 1])
    accum = bacc_ref[...] + grad * grad
    nba[...] = accum
    nb[...] = bias_ref[...] - step_rate * grad / jnp.sqrt(accum)


def update(total, add_a, add_b, vecs, bias, accum, bias_accum, bias_lane, scale):
    row = lambda a: a.reshape(1, ROWS)
    if add_b is None:
        kernel = lambda t, a, *rest: update_kernel(bias_lane, scale, t, a, None, *rest)
        sums = (total, add_a)
    else:
        kernel = functools.partial(update_kernel, bias_lane, scale)
        sums = (total, add_a, add_b)
    f32 = jnp.float32
    nv, nb, na, nba = pl.pallas_call(
        kernel,
        out_shape=[
            jax.ShapeDtypeStruct((ROWS, D), f32),
            jax.ShapeDtypeStruct((1, ROWS), f32),
            jax.ShapeDtypeStruct((ROWS, D), f32),
            jax.ShapeDtypeStruct((1, ROWS), f32),
        ],
        compiler_params=pltpu.CompilerParams(vmem_limit_bytes=6 * MIB),
        cost_estimate=pl.CostEstimate(flops=400000, bytes_accessed=800000, transcendentals=30000),
    )(*sums, vecs, row(bias), accum, row(bias_accum))
    return nv, nb.reshape(ROWS), na, nba.reshape(ROWS)


def spread(index):
    q, p = index // 16, index % 16
    return q // 8, q // 2 % 4, q % 2, p // 4, p % 4


def place(zl, x, c, y, z):
    return (zl % 2 * 8 + x % 4 * 2 + c % 2) * 16 + y % 4 * 4 + z % 4


def move(value, axis):
    perm = []
    for i in range(256):
        zl, x, c, y, z = spread(i)
        s = 1 - 2 * c
        to = {
            "core": (zl, x, c + 1, y, z),
            "zl": (zl + 1, x, c, y, z),
            "x": (zl, x + s, c, y, z),
            "y": (zl, x, c, y + s, z),
            "z": (zl, x, c, y, z + s),
        }[axis]
        perm.append((i, place(*to)))
    return lax.ppermute(value, ("word", "ctx"), perm)


def keep(arrays):
    return [pltpu.with_memory_space_constraint(v, pltpu.VMEM) for v in arrays]


def per_device(
    counts,
    word_vecs,
    word_bias,
    word_accum,
    word_bias_accum,
    ctx_vecs,
    ctx_bias,
    ctx_accum,
    ctx_bias_accum,
):
    f32, low = jnp.float32, jnp.bfloat16
    go = lambda value, axis: move(value, axis)

    word_block, ctx_block, row_index, piece_index, result_index = pack(word_vecs, word_bias, ctx_vecs, ctx_bias)

    both = jnp.stack([word_block, go(word_block, "core")])
    pair = jnp.stack([ctx_block, go(ctx_block, "zl")])
    zr1 = go(both, "z")
    four = jnp.concatenate([pair, go(pair, "core")])
    zr2 = go(zr1[:1], "z")
    xr1 = go(four, "x")
    e1 = go(jnp.concatenate([zr1[1:], zr1[:1], zr2]), "core")
    wy = jnp.concatenate([both[:1], e1[:1], zr2, zr1[:1], both[1:], zr1[1:], e1[2:], e1[1:2]])
    yr1 = go(wy, "y")
    xr2 = go(xr1[:2], "x")
    c0 = jnp.concatenate([four, xr1, xr2])
    c1 = go(c0[4:], "core")
    w2 = go(yr1[:4], "y")
    w1 = go(yr1[4:], "core")

    k0, l0 = keep(weights((0,), row_index, counts))
    k3, l3 = keep(weights((3,), row_index, counts))
    k1, l1, k2, l2 = keep(weights((1, 2), row_index, counts))
    scaled_shape, words_t_shape = low_shape(CHUNK, COLUMNS), low_shape(384, CHUNK)
    g3, s3, t3, ctx_full, ctx_t = call(
        first_kernel, (piece_index,), (yr1, c0, c1, k3, l3),
        [blocks_shape(4, low), scaled_shape, words_t_shape, low_shape(COLUMNS, 384), low_shape(384, COLUMNS)],
        WORDS_SCRATCH, CHUNK_FLOPS, 16,
    )

    def chunk(w, weight, log_count, dtype):
        return call(
            chunk_kernel, (), (w, weight, log_count, ctx_full, ctx_t),
            [blocks_shape(4, dtype), scaled_shape, words_t_shape], WORDS_SCRATCH, CHUNK_FLOPS, 16,
        )

    g1, s1, t1 = chunk(w1, k1, l1, low)
    g2, s2, t2 = chunk(w2, k2, l2, low)
    g0, s0, t0 = chunk(wy, k0, l0, f32)
    h_own, h_other = call(
        ctx_kernel, (result_index,), (s0, s1, s2, s3, t0, t1, t2, t3),
        [blocks_shape(8, f32), blocks_shape(8, low)],
        [pltpu.VMEM((384, COLUMNS), f32), pltpu.VMEM((COLUMNS, 384), f32)], 2 * CHUNK_FLOPS, 16,
    )

    f1 = go(g3, "core")
    ya = go(g2, "y")
    rn = go(jnp.concatenate([g1, f1]), "y")
    hc = go(h_other, "core")
    ya2 = go(ya, "y")
    s = h_own + hc.astype(f32)
    xa, x3 = go(s[4:6].astype(low), "x"), go(s[6:8].astype(low), "core")
    f2 = go(rn[4:], "core")
    z_own, z_next, z_far, z_back = call(
        sum_kernel, (), (g0, rn, f2, ya2),
        [jax.ShapeDtypeStruct((BLOCK, LO), f32)] * 2 + [low_shape(BLOCK, LO)] * 2, [], 4 * BLOCK * LO * 4, 8,
    )
    za, f3 = go(z_far, "z"), go(z_back, "core")
    xr = go(jnp.concatenate([(s[2:4] + xa.astype(f32)).astype(low), x3]), "x")
    x4 = go(xr[2:], "core")
    rz = go(jnp.stack([(z_next + za.astype(f32)).astype(low), f3]), "z")
    t = s[:2] + xr[:2].astype(f32) + x4.astype(f32)
    rl = go(t[1].astype(low), "zl")
    f4 = go(rz[1], "core")

    word_scale = 2.0 / (counts.shape[1] * lax.axis_size("ctx"))
    ctx_scale = 2.0 / (counts.shape[0] * lax.axis_size("word"))
    new_ctx_vecs, new_ctx_bias, new_ctx_accum, new_ctx_bias_accum = update(
        t[0], rl, None, ctx_vecs, ctx_bias, ctx_accum, ctx_bias_accum, D - LO + 1, ctx_scale
    )
    new_word_vecs, new_word_bias, new_word_accum, new_word_bias_accum = update(
        z_own, rz, f4, word_vecs, word_bias, word_accum, word_bias_accum, D - LO, word_scale
    )
    return (
        new_word_vecs,
        new_word_bias,
        new_word_accum,
        new_word_bias_accum,
        new_ctx_vecs,
        new_ctx_bias,
        new_ctx_accum,
        new_ctx_bias_accum,
    )


def solution(mesh):
    words, contexts = P(("word", "ctx")), P(("ctx", "word"))
    return jax.shard_map(
        per_device,
        mesh=mesh,
        in_specs=(P("word", "ctx"), words, words, words, words, contexts, contexts, contexts, contexts),
        out_specs=(words, words, words, words, contexts, contexts, contexts, contexts),
        check_vma=False,
    )
```

```python
import functools
import math

import jax
import jax.numpy as jnp
from jax import lax
from jax.experimental import pallas as pl
from jax.experimental.pallas import tpu as pltpu
from jax.sharding import PartitionSpec as P


count_cap = 100.0
power_law = 0.75
step_rate = 0.2

ROWS = 96
BLOCK = 120
D = 300
LO = 256
USED = 320
MIB = 1 << 20


def pack_rows(main, tail):
    lane = lax.broadcasted_iota(jnp.int32, (24, 128), 1)
    low = lane < 64
    t = [tail[24 * g : 24 * g + 24, :] for g in range(4)]
    left = jnp.where(low, t[0], pltpu.roll(t[1], 64, 1))
    right = jnp.where(low, t[2], pltpu.roll(t[3], 64, 1))
    return jnp.concatenate([main, jnp.concatenate([left, right], axis=1)], axis=0)


def unpack_tail(packed):
    left, right = packed[ROWS:BLOCK, :128], packed[ROWS:BLOCK, 128:]
    return jnp.concatenate([left, pltpu.roll(left, 64, 1), right, pltpu.roll(right, 64, 1)], axis=0)


def to_column(row):
    eye = lax.broadcasted_iota(jnp.int32, (ROWS, ROWS), 0) == lax.broadcasted_iota(jnp.int32, (ROWS, ROWS), 1)
    return jnp.sum(jnp.where(eye, jnp.broadcast_to(row, (ROWS, ROWS)), 0.0), axis=1, keepdims=True)


def to_row(column):
    eye = lax.broadcasted_iota(jnp.int32, (ROWS, ROWS), 0) == lax.broadcasted_iota(jnp.int32, (ROWS, ROWS), 1)
    return jnp.sum(jnp.where(eye, jnp.broadcast_to(column, (ROWS, ROWS)), 0.0), axis=0, keepdims=True)


def pack_one(bias_lane, vec_ref, bias_ref, out_ref, tail_ref):
    tail_ref[...] = jnp.zeros_like(tail_ref)
    tail_ref[:, : D - LO] = vec_ref[:, LO:]
    lane = lax.broadcasted_iota(jnp.int32, (ROWS, 128), 1)
    tail = jnp.where(lane == bias_lane, jnp.broadcast_to(to_column(bias_ref[...]), (ROWS, 128)), tail_ref[...])
    out_ref[...] = pack_rows(vec_ref[:, :LO], tail).astype(jnp.bfloat16)


PIECES = (
    (0, 0, 0), (0, 0, 1), (1, 0, 0), (1, 0, 1), (0, -1, 0), (0, -1, 1), (1, -1, 0), (1, -1, 1), (0, 2, 0), (0, 2, 1),
    (1, 1, 0), (1, 1, 1), (0, 1, 0), (0, 1, 1), (1, 2, 0), (1, 2, 1),
)
RESULTS = tuple(
    (d, b, a) for d, b in ((0, 0), (0, 1), (1, 1), (0, 2), (1, 0), (1, -1), (0, -1), (1, 2)) for a in (0, 1)
)


def pack_kernel(wv, wb, cv, cb, word_out, ctx_out, row_index, piece_index, result_index, tail_ref):
    p, q = lax.axis_index("ctx"), lax.axis_index("word")
    y, z = lax.div(p, 4), lax.rem(p, 4)
    zl, x, c = lax.div(q, 8), lax.rem(lax.div(q, 2), 4), lax.rem(q, 2)
    s = 1 - 2 * c
    for k in range(4):
        for j in range(4):
            row_index[4 * k + j] = lax.rem(y + k * s + 4, 4) * 4 + lax.rem(z + j * s + 4, 4)
    for out, table in ((piece_index, PIECES), (result_index, RESULTS)):
        for i, (d, b, a) in enumerate(table):
            out[i] = lax.rem(zl + a, 2) * 8 + lax.rem(x + b * s + 4, 4) * 2 + lax.rem(c + d, 2)
    pack_one(D - LO, wv, wb, word_out, tail_ref)
    pack_one(D - LO + 1, cv, cb, ctx_out, tail_ref)


def pack(word_vecs, word_bias, ctx_vecs, ctx_bias):
    return pl.pallas_call(
        pack_kernel,
        out_specs=[pl.BlockSpec(memory_space=pltpu.VMEM)] * 2 + [pl.BlockSpec(memory_space=pltpu.SMEM)] * 3,
        out_shape=[jax.ShapeDtypeStruct((BLOCK, LO), jnp.bfloat16)] * 2 + [jax.ShapeDtypeStruct((16,), jnp.int32)] * 3,
        scratch_shapes=[pltpu.VMEM((ROWS, 128), jnp.float32)],
        compiler_params=pltpu.CompilerParams(vmem_limit_bytes=4 * MIB),
        cost_estimate=pl.CostEstimate(flops=100000, bytes_accessed=400000, transcendentals=0),
        name="pack",
    )(*(pltpu.with_memory_space_constraint(v, pltpu.HBM) for v in (word_vecs, word_bias.reshape(1, ROWS), ctx_vecs, ctx_bias.reshape(1, ROWS))))


def weight_kernel(chunks, index_ref, counts, *refs):
    outs, (held, sems) = refs[:-2], refs[-2:]

    def fetch(n):
        start = pl.multiple_of(index_ref[4 * chunks[n // 4] + n % 4] * ROWS, ROWS)
        return pltpu.make_async_copy(counts.at[pl.ds(start, ROWS)], held.at[n], sems.at[n])

    copies = [fetch(n) for n in range(4 * len(chunks))]
    for copy in copies:
        copy.start()
    for n, copy in enumerate(copies):
        weight_ref, log_ref = outs[n // 4 * 2], outs[n // 4 * 2 + 1]
        copy.wait()

        def step(i, _):
            rows = pl.ds(pl.multiple_of(i * 8, 8), 8)
            count = held[n, rows, :]
            log_count = jnp.log(jnp.maximum(count.astype(jnp.float32), 1.0))
            exponent = log_count * (power_law / math.log(2.0)) - power_law * math.log2(count_cap)
            power = jnp.exp2(jnp.minimum(exponent, 0.0))
            to = pl.ds(pl.multiple_of(n % 4 * ROWS + i * 8, 8), 8)
            weight_ref[to, :] = jnp.where(count > 0, power, 0.0)
            log_ref[to, :] = log_count
            return 0

        lax.fori_loop(0, ROWS // 8, step, 0, unroll=3)


def weights(chunks, index, counts):
    columns, n = counts.shape[1], len(chunks)
    return pl.pallas_call(
        functools.partial(weight_kernel, chunks),
        in_specs=[pl.BlockSpec(memory_space=pltpu.SMEM), pl.BlockSpec(memory_space=pltpu.HBM)],
        out_specs=[pl.BlockSpec(memory_space=pltpu.VMEM)] * (2 * n),
        out_shape=[pltpu.VMEM((4 * ROWS, columns), jnp.float32)] * (2 * n),
        scratch_shapes=[pltpu.VMEM((4 * n, ROWS, columns), jnp.int32), pltpu.SemaphoreType.DMA((4 * n,))],
        compiler_params=pltpu.CompilerParams(vmem_limit_bytes=8 * MIB),
        cost_estimate=pl.CostEstimate(
            flops=80 * n * ROWS * columns, bytes_accessed=48 * n * ROWS * columns, transcendentals=8 * n * ROWS * columns
        ),
    )(index, pltpu.with_memory_space_constraint(counts, pltpu.HBM))


def rows_of(index_ref, i):
    return pl.ds(pl.multiple_of(index_ref[i] * ROWS, ROWS), ROWS)


def word_chunk(blocks, weight, log_count, ctx_full, ctx_t, words, words_t, scaled_ref):
    lane = lax.broadcasted_iota(jnp.int32, (ROWS, 128), 1)
    bc = D - LO + 1
    for j in range(4):
        packed = blocks[j].astype(jnp.float32)
        tail = unpack_tail(packed)
        tail = jnp.where(lane < bc, tail, jnp.where(lane == bc, 1.0, 0.0))
        words[ROWS * j : ROWS * j + ROWS, :LO] = packed[:ROWS].astype(jnp.bfloat16)
        words[ROWS * j : ROWS * j + ROWS, LO:] = tail.astype(jnp.bfloat16)
    word_rows = words[...]
    words_t[...] = word_rows.T
    inner = jnp.dot(word_rows, ctx_t[...], preferred_element_type=jnp.float32)
    scaled_ref[...] = (weight[...] * (inner - log_count[...])).astype(jnp.bfloat16)
    term = jnp.dot(scaled_ref[...], ctx_full[...], preferred_element_type=jnp.float32)
    parts = [term[ROWS * j : ROWS * j + ROWS] for j in range(4)]
    return [pack_rows(part[:, :LO], part[:, LO:]) for part in parts]


def build(index_ref, c0, c1, ctx_full, ctx_t):
    lane = lax.broadcasted_iota(jnp.int32, (ROWS, 128), 1)
    bw, bc = D - LO, D - LO + 1
    for i in range(16):
        packed = (c0[i] if i < 10 else c1[i - 10]).astype(jnp.float32)
        tail = unpack_tail(packed)
        tail = jnp.where(lane == bw, 1.0, jnp.where(lane <= bc, tail, 0.0))
        ctx_full[rows_of(index_ref, i), :LO] = packed[:ROWS].astype(jnp.bfloat16)
        ctx_full[rows_of(index_ref, i), LO:] = tail.astype(jnp.bfloat16)
    ctx_t[...] = ctx_full[...].T


def chunk_kernel(w, weight, log_count, ctx_full, ctx_t, grad, scaled, words_t, words):
    blocks = [w[j] for j in range(4)]
    for j, packed in enumerate(word_chunk(blocks, weight, log_count, ctx_full, ctx_t, words, words_t, scaled)):
        grad[j] = packed.astype(grad.dtype)


def first_kernel(index_ref, w, c0, c1, weight, log_count, grad, scaled, words_t, ctx_full, ctx_t, words):
    build(index_ref, c0, c1, ctx_full, ctx_t)
    chunk_kernel(w, weight, log_count, ctx_full, ctx_t, grad, scaled, words_t, words)


def ctx_kernel(index_ref, s0, s1, s2, s3, t0, t1, t2, t3, h_own, h_other, ctx_grad, back):
    for k, (t, s) in enumerate(((t0, s0), (t1, s1), (t2, s2), (t3, s3))):
        term = jnp.dot(t[:USED, :], s[...], preferred_element_type=jnp.float32)
        ctx_grad[:USED, :] = term if k == 0 else ctx_grad[:USED, :] + term
    back[...] = ctx_grad[...].T
    for i in range(16):
        term = back[rows_of(index_ref, i), :]
        packed = pack_rows(term[:, :LO], term[:, LO:])
        if i < 8:
            h_own[i] = packed
        else:
            h_other[i - 8] = packed.astype(jnp.bfloat16)


def sum_kernel(g0, rn, f2, ya, own, nxt, far, back):
    f32 = jnp.float32
    for j, out in enumerate((own, nxt, far, back)):
        total = g0[j] + rn[j].astype(f32) + f2[j].astype(f32) + ya[j].astype(f32)
        out[...] = total.astype(out.dtype)


def last_kernel(s, xr, x4, own, far):
    for j, out in enumerate((own, far)):
        out[...] = (s[j] + xr[j].astype(jnp.float32) + x4[j].astype(jnp.float32)).astype(out.dtype)


CHUNK, COLUMNS = 4 * ROWS, 16 * ROWS
SMEM_SPEC = pl.BlockSpec(memory_space=pltpu.SMEM)
VMEM_SPEC = pl.BlockSpec(memory_space=pltpu.VMEM)


def blocks_shape(n, dtype):
    return jax.ShapeDtypeStruct((n, BLOCK, LO), dtype)


def low_shape(*dims):
    return jax.ShapeDtypeStruct(dims, jnp.bfloat16)


def call(kernel, scalars, operands, out_shape, scratch, flops, limit):
    return pl.pallas_call(
        kernel,
        in_specs=[SMEM_SPEC] * len(scalars) + [VMEM_SPEC] * len(operands),
        out_specs=[VMEM_SPEC] * len(out_shape),
        out_shape=out_shape,
        scratch_shapes=scratch,
        compiler_params=pltpu.CompilerParams(vmem_limit_bytes=limit * MIB),
        cost_estimate=pl.CostEstimate(flops=flops, bytes_accessed=4 * MIB, transcendentals=0),
    )(*scalars, *operands)


CHUNK_FLOPS = 4 * CHUNK * COLUMNS * 384
WORDS_SCRATCH = [pltpu.VMEM((CHUNK, 384), jnp.bfloat16)]


def update_kernel(bias_lane, scale, total_ref, add_a, add_b, vec_ref, bias_ref, acc_ref, bacc_ref, nv, nb, na, nba):
    packed = total_ref[...] + (add_a[0] if len(add_a.shape) == 3 else add_a[...]).astype(jnp.float32)
    if add_b is not None:
        packed = packed + add_b[...].astype(jnp.float32)
    packed = packed * scale
    tail = unpack_tail(packed)
    for columns, grad in ((slice(0, LO), packed[:ROWS]), (slice(LO, D), tail[:, : D - LO])):
        accum = acc_ref[:, columns] + grad * grad
        na[:, columns] = accum
        nv[:, columns] = vec_ref[:, columns] - step_rate * grad / jnp.sqrt(accum)
    grad = to_row(tail[:, bias_lane : bias_lane + 1])
    accum = bacc_ref[...] + grad * grad
    nba[...] = accum
    nb[...] = bias_ref[...] - step_rate * grad / jnp.sqrt(accum)


def update(total, add_a, add_b, vecs, bias, accum, bias_accum, bias_lane, scale):
    row = lambda a: a.reshape(1, ROWS)
    if add_b is None:
        kernel = lambda t, a, *rest: update_kernel(bias_lane, scale, t, a, None, *rest)
        sums = (total, add_a)
    else:
        kernel = functools.partial(update_kernel, bias_lane, scale)
        sums = (total, add_a, add_b)
    f32 = jnp.float32
    nv, nb, na, nba = pl.pallas_call(
        kernel,
        out_shape=[
            jax.ShapeDtypeStruct((ROWS, D), f32),
            jax.ShapeDtypeStruct((1, ROWS), f32),
            jax.ShapeDtypeStruct((ROWS, D), f32),
            jax.ShapeDtypeStruct((1, ROWS), f32),
        ],
        compiler_params=pltpu.CompilerParams(vmem_limit_bytes=6 * MIB),
        cost_estimate=pl.CostEstimate(flops=400000, bytes_accessed=800000, transcendentals=30000),
    )(*sums, vecs, row(bias), accum, row(bias_accum))
    return nv, nb.reshape(ROWS), na, nba.reshape(ROWS)


def spread(index):
    q, p = index // 16, index % 16
    return q // 8, q // 2 % 4, q % 2, p // 4, p % 4


def place(zl, x, c, y, z):
    return (zl % 2 * 8 + x % 4 * 2 + c % 2) * 16 + y % 4 * 4 + z % 4


def move(value, axis):
    perm = []
    for i in range(256):
        zl, x, c, y, z = spread(i)
        s = 1 - 2 * c
        to = {
            "core": (zl, x, c + 1, y, z),
            "zl": (zl + 1, x, c, y, z),
            "x": (zl, x + s, c, y, z),
            "y": (zl, x, c, y + s, z),
            "z": (zl, x, c, y, z + s),
        }[axis]
        perm.append((i, place(*to)))
    return lax.ppermute(value, ("word", "ctx"), perm)


def keep(arrays):
    return [pltpu.with_memory_space_constraint(v, pltpu.VMEM) for v in arrays]


def per_device(
    counts,
    word_vecs,
    word_bias,
    word_accum,
    word_bias_accum,
    ctx_vecs,
    ctx_bias,
    ctx_accum,
    ctx_bias_accum,
):
    f32, low = jnp.float32, jnp.bfloat16
    go = lambda value, axis: move(value, axis)

    word_block, ctx_block, row_index, piece_index, result_index = pack(word_vecs, word_bias, ctx_vecs, ctx_bias)

    both = jnp.stack([word_block, go(word_block, "core")])
    pair = jnp.stack([ctx_block, go(ctx_block, "zl")])
    zr1 = go(both, "z")
    four = jnp.concatenate([pair, go(pair, "core")])
    zr2 = go(zr1[:1], "z")
    xr1 = go(four, "x")
    e1 = go(jnp.concatenate([zr1[1:], zr1[:1], zr2]), "core")
    wy = jnp.concatenate([both[:1], e1[:1], zr2, zr1[:1], both[1:], zr1[1:], e1[2:], e1[1:2]])
    yr1 = go(wy, "y")
    xr2 = go(xr1[:2], "x")
    c0 = jnp.concatenate([four, xr1, xr2])
    c1 = go(c0[4:], "core")
    w2 = go(yr1[:4], "y")
    w1 = go(yr1[4:], "core")

    k0, l0 = keep(weights((0,), row_index, counts))
    k3, l3 = keep(weights((3,), row_index, counts))
    k1, l1, k2, l2 = keep(weights((1, 2), row_index, counts))
    scaled_shape, words_t_shape = low_shape(CHUNK, COLUMNS), low_shape(384, CHUNK)
    g3, s3, t3, ctx_full, ctx_t = call(
        first_kernel, (piece_index,), (yr1, c0, c1, k3, l3),
        [blocks_shape(4, low), scaled_shape, words_t_shape, low_shape(COLUMNS, 384), low_shape(384, COLUMNS)],
        WORDS_SCRATCH, CHUNK_FLOPS, 16,
    )

    def chunk(w, weight, log_count, dtype):
        return call(
            chunk_kernel, (), (w, weight, log_count, ctx_full, ctx_t),
            [blocks_shape(4, dtype), scaled_shape, words_t_shape], WORDS_SCRATCH, CHUNK_FLOPS, 16,
        )

    g1, s1, t1 = chunk(w1, k1, l1, low)
    g2, s2, t2 = chunk(w2, k2, l2, low)
    g0, s0, t0 = chunk(wy, k0, l0, f32)
    h_own, h_other = call(
        ctx_kernel, (result_index,), (s0, s1, s2, s3, t0, t1, t2, t3),
        [blocks_shape(8, f32), blocks_shape(8, low)],
        [pltpu.VMEM((384, COLUMNS), f32), pltpu.VMEM((COLUMNS, 384), f32)], 2 * CHUNK_FLOPS, 16,
    )

    f1 = go(g3, "core")
    ya = go(g2, "y")
    rn = go(jnp.concatenate([g1, f1]), "y")
    hc = go(h_other, "core")
    ya2 = go(ya, "y")
    s = h_own + hc.astype(f32)
    xa = go(s[6:].astype(low), "x")
    f2 = go(rn[4:], "core")
    z_own, z_next, z_far, z_back = call(
        sum_kernel, (), (g0, rn, f2, ya2),
        [jax.ShapeDtypeStruct((BLOCK, LO), f32)] * 2 + [low_shape(BLOCK, LO)] * 2, [], 4 * BLOCK * LO * 4, 8,
    )
    za, f3 = go(z_far, "z"), go(z_back, "core")
    xr = go(jnp.concatenate([s[2:4] + xa.astype(f32), s[4:6]]).astype(low), "x")
    x4 = go(xr[2:], "core")
    rz = go(jnp.stack([(z_next + za.astype(f32)).astype(low), f3]), "z")
    t_own, t_far = call(
        last_kernel, (), (s, xr, x4), [jax.ShapeDtypeStruct((BLOCK, LO), f32), low_shape(BLOCK, LO)],
        [], 4 * BLOCK * LO, 8,
    )
    rl = go(t_far, "zl")
    f4 = go(rz[1], "core")

    word_scale = 2.0 / (counts.shape[1] * lax.axis_size("ctx"))
    ctx_scale = 2.0 / (counts.shape[0] * lax.axis_size("word"))
    new_ctx_vecs, new_ctx_bias, new_ctx_accum, new_ctx_bias_accum = update(
        t_own, rl, None, ctx_vecs, ctx_bias, ctx_accum, ctx_bias_accum, D - LO + 1, ctx_scale
    )
    new_word_vecs, new_word_bias, new_word_accum, new_word_bias_accum = update(
        z_own, rz, f4, word_vecs, word_bias, word_accum, word_bias_accum, D - LO, word_scale
    )
    return (
        new_word_vecs,
        new_word_bias,
        new_word_accum,
        new_word_bias_accum,
        new_ctx_vecs,
        new_ctx_bias,
        new_ctx_accum,
        new_ctx_bias_accum,
    )


def solution(mesh):
    words, contexts = P(("word", "ctx")), P(("ctx", "word"))
    return jax.shard_map(
        per_device,
        mesh=mesh,
        in_specs=(P("word", "ctx"), words, words, words, words, contexts, contexts, contexts, contexts),
        out_specs=(words, words, words, words, contexts, contexts, contexts, contexts),
        check_vma=False,
    )
```

```python
import functools
import math

import jax
import jax.numpy as jnp
from jax import lax
from jax.experimental import pallas as pl
from jax.experimental.pallas import tpu as pltpu
from jax.sharding import PartitionSpec as P


count_cap = 100.0
power_law = 0.75
step_rate = 0.2

ROWS = 96
BLOCK = 120
D = 300
LO = 256
USED = 320
MIB = 1 << 20


def pack_rows(main, tail):
    lane = lax.broadcasted_iota(jnp.int32, (24, 128), 1)
    low = lane < 64
    t = [tail[24 * g : 24 * g + 24, :] for g in range(4)]
    left = jnp.where(low, t[0], pltpu.roll(t[1], 64, 1))
    right = jnp.where(low, t[2], pltpu.roll(t[3], 64, 1))
    return jnp.concatenate([main, jnp.concatenate([left, right], axis=1)], axis=0)


def unpack_tail(packed):
    left, right = packed[ROWS:BLOCK, :128], packed[ROWS:BLOCK, 128:]
    return jnp.concatenate([left, pltpu.roll(left, 64, 1), right, pltpu.roll(right, 64, 1)], axis=0)


def to_column(row):
    eye = lax.broadcasted_iota(jnp.int32, (ROWS, ROWS), 0) == lax.broadcasted_iota(jnp.int32, (ROWS, ROWS), 1)
    return jnp.sum(jnp.where(eye, jnp.broadcast_to(row, (ROWS, ROWS)), 0.0), axis=1, keepdims=True)


def to_row(column):
    eye = lax.broadcasted_iota(jnp.int32, (ROWS, ROWS), 0) == lax.broadcasted_iota(jnp.int32, (ROWS, ROWS), 1)
    return jnp.sum(jnp.where(eye, jnp.broadcast_to(column, (ROWS, ROWS)), 0.0), axis=0, keepdims=True)


def pack_one(bias_lane, vec_ref, bias_ref, out_ref, tail_ref):
    tail_ref[...] = jnp.zeros_like(tail_ref)
    tail_ref[:, : D - LO] = vec_ref[:, LO:]
    lane = lax.broadcasted_iota(jnp.int32, (ROWS, 128), 1)
    tail = jnp.where(lane == bias_lane, jnp.broadcast_to(to_column(bias_ref[...]), (ROWS, 128)), tail_ref[...])
    out_ref[...] = pack_rows(vec_ref[:, :LO], tail).astype(jnp.bfloat16)


PIECES = (
    (0, 0, 0), (0, 0, 1), (1, 0, 0), (1, 0, 1), (0, -1, 0), (0, -1, 1), (1, -1, 0), (1, -1, 1), (0, 2, 0), (0, 2, 1),
    (1, 1, 0), (1, 1, 1), (0, 1, 0), (0, 1, 1), (1, 2, 0), (1, 2, 1),
)
RESULTS = tuple(
    (d, b, a) for d, b in ((0, 0), (0, 1), (1, 1), (0, 2), (1, 0), (1, -1), (0, -1), (1, 2)) for a in (0, 1)
)


def pack_kernel(wv, wb, cv, cb, word_out, ctx_out, row_index, piece_index, result_index, tail_ref):
    p, q = lax.axis_index("ctx"), lax.axis_index("word")
    y, z = lax.div(p, 4), lax.rem(p, 4)
    zl, x, c = lax.div(q, 8), lax.rem(lax.div(q, 2), 4), lax.rem(q, 2)
    s = 1 - 2 * c
    for k in range(4):
        for j in range(4):
            row_index[4 * k + j] = lax.rem(y + k * s + 4, 4) * 4 + lax.rem(z + j * s + 4, 4)
    for out, table in ((piece_index, PIECES), (result_index, RESULTS)):
        for i, (d, b, a) in enumerate(table):
            out[i] = lax.rem(zl + a, 2) * 8 + lax.rem(x + b * s + 4, 4) * 2 + lax.rem(c + d, 2)
    pack_one(D - LO, wv, wb, word_out, tail_ref)
    pack_one(D - LO + 1, cv, cb, ctx_out, tail_ref)


def pack(word_vecs, word_bias, ctx_vecs, ctx_bias):
    return pl.pallas_call(
        pack_kernel,
        out_specs=[pl.BlockSpec(memory_space=pltpu.VMEM)] * 2 + [pl.BlockSpec(memory_space=pltpu.SMEM)] * 3,
        out_shape=[jax.ShapeDtypeStruct((BLOCK, LO), jnp.bfloat16)] * 2 + [jax.ShapeDtypeStruct((16,), jnp.int32)] * 3,
        scratch_shapes=[pltpu.VMEM((ROWS, 128), jnp.float32)],
        compiler_params=pltpu.CompilerParams(vmem_limit_bytes=4 * MIB),
        cost_estimate=pl.CostEstimate(flops=100000, bytes_accessed=400000, transcendentals=0),
        name="pack",
    )(*(pltpu.with_memory_space_constraint(v, pltpu.HBM) for v in (word_vecs, word_bias.reshape(1, ROWS), ctx_vecs, ctx_bias.reshape(1, ROWS))))


def weight_kernel(chunks, index_ref, counts, *refs):
    outs, (held, sems) = refs[:-2], refs[-2:]

    def fetch(n):
        start = pl.multiple_of(index_ref[4 * chunks[n // 4] + n % 4] * ROWS, ROWS)
        return pltpu.make_async_copy(counts.at[pl.ds(start, ROWS)], held.at[n], sems.at[n])

    copies = [fetch(n) for n in range(4 * len(chunks))]
    for copy in copies:
        copy.start()
    for n, copy in enumerate(copies):
        weight_ref, log_ref = outs[n // 4 * 2], outs[n // 4 * 2 + 1]
        copy.wait()

        def step(i, _):
            rows = pl.ds(pl.multiple_of(i * 8, 8), 8)
            count = held[n, rows, :]
            log_count = jnp.log(jnp.maximum(count.astype(jnp.float32), 1.0))
            exponent = log_count * (power_law / math.log(2.0)) - power_law * math.log2(count_cap)
            power = jnp.exp2(jnp.minimum(exponent, 0.0))
            to = pl.ds(pl.multiple_of(n % 4 * ROWS + i * 8, 8), 8)
            weight_ref[to, :] = jnp.where(count > 0, power, 0.0)
            log_ref[to, :] = log_count
            return 0

        lax.fori_loop(0, ROWS // 8, step, 0, unroll=3)


def weights(chunks, index, counts):
    columns, n = counts.shape[1], len(chunks)
    return pl.pallas_call(
        functools.partial(weight_kernel, chunks),
        in_specs=[pl.BlockSpec(memory_space=pltpu.SMEM), pl.BlockSpec(memory_space=pltpu.HBM)],
        out_specs=[pl.BlockSpec(memory_space=pltpu.VMEM)] * (2 * n),
        out_shape=[pltpu.VMEM((4 * ROWS, columns), jnp.float32)] * (2 * n),
        scratch_shapes=[pltpu.VMEM((4 * n, ROWS, columns), jnp.int32), pltpu.SemaphoreType.DMA((4 * n,))],
        compiler_params=pltpu.CompilerParams(vmem_limit_bytes=8 * MIB),
        cost_estimate=pl.CostEstimate(
            flops=80 * n * ROWS * columns, bytes_accessed=48 * n * ROWS * columns, transcendentals=8 * n * ROWS * columns
        ),
    )(index, pltpu.with_memory_space_constraint(counts, pltpu.HBM))


def rows_of(index_ref, i):
    return pl.ds(pl.multiple_of(index_ref[i] * ROWS, ROWS), ROWS)


def word_chunk(blocks, weight, log_count, ctx_full, ctx_t, words, words_t, scaled_ref):
    lane = lax.broadcasted_iota(jnp.int32, (ROWS, 128), 1)
    bc = D - LO + 1
    for j in range(4):
        packed = blocks[j].astype(jnp.float32)
        tail = unpack_tail(packed)
        tail = jnp.where(lane < bc, tail, jnp.where(lane == bc, 1.0, 0.0))
        words[ROWS * j : ROWS * j + ROWS, :LO] = packed[:ROWS].astype(jnp.bfloat16)
        words[ROWS * j : ROWS * j + ROWS, LO:] = tail.astype(jnp.bfloat16)
    word_rows = words[...]
    words_t[...] = word_rows.T
    inner = jnp.dot(word_rows, ctx_t[...], preferred_element_type=jnp.float32)
    scaled_ref[...] = (weight[...] * (inner - log_count[...])).astype(jnp.bfloat16)
    term = jnp.dot(scaled_ref[...], ctx_full[...], preferred_element_type=jnp.float32)
    parts = [term[ROWS * j : ROWS * j + ROWS] for j in range(4)]
    return [pack_rows(part[:, :LO], part[:, LO:]) for part in parts]


def build(index_ref, c0, c1, ctx_full, ctx_t):
    lane = lax.broadcasted_iota(jnp.int32, (ROWS, 128), 1)
    bw, bc = D - LO, D - LO + 1
    for i in range(16):
        packed = (c0[i] if i < 10 else c1[i - 10]).astype(jnp.float32)
        tail = unpack_tail(packed)
        tail = jnp.where(lane == bw, 1.0, jnp.where(lane <= bc, tail, 0.0))
        ctx_full[rows_of(index_ref, i), :LO] = packed[:ROWS].astype(jnp.bfloat16)
        ctx_full[rows_of(index_ref, i), LO:] = tail.astype(jnp.bfloat16)
    ctx_t[...] = ctx_full[...].T


def chunk_kernel(w, weight, log_count, ctx_full, ctx_t, grad, scaled, words_t, words):
    blocks = [w[j] for j in range(4)]
    for j, packed in enumerate(word_chunk(blocks, weight, log_count, ctx_full, ctx_t, words, words_t, scaled)):
        grad[j] = packed.astype(grad.dtype)


def first_kernel(index_ref, w, c0, c1, weight, log_count, grad, scaled, words_t, ctx_full, ctx_t, words):
    build(index_ref, c0, c1, ctx_full, ctx_t)
    chunk_kernel(w, weight, log_count, ctx_full, ctx_t, grad, scaled, words_t, words)


def ctx_kernel(index_ref, s0, s1, s2, s3, t0, t1, t2, t3, h_own, h_other, ctx_grad, back):
    for k, (t, s) in enumerate(((t0, s0), (t1, s1), (t2, s2), (t3, s3))):
        term = jnp.dot(t[:USED, :], s[...], preferred_element_type=jnp.float32)
        ctx_grad[:USED, :] = term if k == 0 else ctx_grad[:USED, :] + term
    back[...] = ctx_grad[...].T
    for i in range(16):
        term = back[rows_of(index_ref, i), :]
        packed = pack_rows(term[:, :LO], term[:, LO:])
        if i < 8:
            h_own[i] = packed
        else:
            h_other[i - 8] = packed.astype(jnp.bfloat16)


def sum_kernel(g0, rn, f2, ya, own, nxt, far, back):
    f32 = jnp.float32
    for j, out in enumerate((own, nxt, far, back)):
        total = g0[j] + rn[j].astype(f32) + f2[j].astype(f32) + ya[j].astype(f32)
        out[...] = total.astype(out.dtype)


def near_kernel(s, xa, _, out):
    for j in range(4):
        out[j] = (s[2 + j] + xa[j].astype(jnp.float32) if j < 2 else s[2 + j]).astype(jnp.bfloat16)


def last_kernel(s, xr, x4, own, far):
    for j, out in enumerate((own, far)):
        out[...] = (s[j] + xr[j].astype(jnp.float32) + x4[j].astype(jnp.float32)).astype(out.dtype)


CHUNK, COLUMNS = 4 * ROWS, 16 * ROWS
SMEM_SPEC = pl.BlockSpec(memory_space=pltpu.SMEM)
VMEM_SPEC = pl.BlockSpec(memory_space=pltpu.VMEM)


def blocks_shape(n, dtype):
    return jax.ShapeDtypeStruct((n, BLOCK, LO), dtype)


def low_shape(*dims):
    return jax.ShapeDtypeStruct(dims, jnp.bfloat16)


def call(kernel, scalars, operands, out_shape, scratch, flops, limit):
    return pl.pallas_call(
        kernel,
        in_specs=[SMEM_SPEC] * len(scalars) + [VMEM_SPEC] * len(operands),
        out_specs=[VMEM_SPEC] * len(out_shape),
        out_shape=out_shape,
        scratch_shapes=scratch,
        compiler_params=pltpu.CompilerParams(vmem_limit_bytes=limit * MIB),
        cost_estimate=pl.CostEstimate(flops=flops, bytes_accessed=4 * MIB, transcendentals=0),
    )(*scalars, *operands)


CHUNK_FLOPS = 4 * CHUNK * COLUMNS * 384
WORDS_SCRATCH = [pltpu.VMEM((CHUNK, 384), jnp.bfloat16)]


def update_kernel(bias_lane, scale, total_ref, add_a, add_b, vec_ref, bias_ref, acc_ref, bacc_ref, nv, nb, na, nba):
    packed = total_ref[...] + (add_a[0] if len(add_a.shape) == 3 else add_a[...]).astype(jnp.float32)
    if add_b is not None:
        packed = packed + add_b[...].astype(jnp.float32)
    packed = packed * scale
    tail = unpack_tail(packed)
    for columns, grad in ((slice(0, LO), packed[:ROWS]), (slice(LO, D), tail[:, : D - LO])):
        accum = acc_ref[:, columns] + grad * grad
        na[:, columns] = accum
        nv[:, columns] = vec_ref[:, columns] - step_rate * grad / jnp.sqrt(accum)
    grad = to_row(tail[:, bias_lane : bias_lane + 1])
    accum = bacc_ref[...] + grad * grad
    nba[...] = accum
    nb[...] = bias_ref[...] - step_rate * grad / jnp.sqrt(accum)


def update(total, add_a, add_b, vecs, bias, accum, bias_accum, bias_lane, scale):
    row = lambda a: a.reshape(1, ROWS)
    if add_b is None:
        kernel = lambda t, a, *rest: update_kernel(bias_lane, scale, t, a, None, *rest)
        sums = (total, add_a)
    else:
        kernel = functools.partial(update_kernel, bias_lane, scale)
        sums = (total, add_a, add_b)
    f32 = jnp.float32
    nv, nb, na, nba = pl.pallas_call(
        kernel,
        out_shape=[
            jax.ShapeDtypeStruct((ROWS, D), f32),
            jax.ShapeDtypeStruct((1, ROWS), f32),
            jax.ShapeDtypeStruct((ROWS, D), f32),
            jax.ShapeDtypeStruct((1, ROWS), f32),
        ],
        compiler_params=pltpu.CompilerParams(vmem_limit_bytes=6 * MIB),
        cost_estimate=pl.CostEstimate(flops=400000, bytes_accessed=800000, transcendentals=30000),
    )(*sums, vecs, row(bias), accum, row(bias_accum))
    return nv, nb.reshape(ROWS), na, nba.reshape(ROWS)


def spread(index):
    q, p = index // 16, index % 16
    return q // 8, q // 2 % 4, q % 2, p // 4, p % 4


def place(zl, x, c, y, z):
    return (zl % 2 * 8 + x % 4 * 2 + c % 2) * 16 + y % 4 * 4 + z % 4


def move(value, axis):
    perm = []
    for i in range(256):
        zl, x, c, y, z = spread(i)
        s = 1 - 2 * c
        to = {
            "core": (zl, x, c + 1, y, z),
            "zl": (zl + 1, x, c, y, z),
            "x": (zl, x + s, c, y, z),
            "y": (zl, x, c, y + s, z),
            "z": (zl, x, c, y, z + s),
        }[axis]
        perm.append((i, place(*to)))
    return lax.ppermute(value, ("word", "ctx"), perm)


def keep(arrays):
    return [pltpu.with_memory_space_constraint(v, pltpu.VMEM) for v in arrays]


def per_device(
    counts,
    word_vecs,
    word_bias,
    word_accum,
    word_bias_accum,
    ctx_vecs,
    ctx_bias,
    ctx_accum,
    ctx_bias_accum,
):
    f32, low = jnp.float32, jnp.bfloat16
    go = lambda value, axis: move(value, axis)

    word_block, ctx_block, row_index, piece_index, result_index = pack(word_vecs, word_bias, ctx_vecs, ctx_bias)

    both = jnp.stack([word_block, go(word_block, "core")])
    pair = jnp.stack([ctx_block, go(ctx_block, "zl")])
    zr1 = go(both, "z")
    y1a = go(both, "y")
    four = jnp.concatenate([pair, go(pair, "core")])
    zr2 = go(zr1[:1], "z")
    xr1 = go(four, "x")
    y1b = go(zr1, "y")
    e1 = go(jnp.concatenate([zr1[1:], zr1[:1], zr2]), "core")
    y1c = go(jnp.concatenate([e1, zr2]), "y")
    xr2 = go(xr1[:2], "x")
    c0 = jnp.concatenate([four, xr1, xr2])
    c1 = go(c0[4:], "core")
    w0 = jnp.concatenate([both[:1], e1[:1], zr2, zr1[:1]])
    w3 = jnp.concatenate([y1a[:1], y1c[:1], y1c[3:], y1b[:1]])
    w2 = go(w3, "y")
    w1 = go(jnp.concatenate([y1a[1:], y1b[1:], y1c[2:3], y1c[1:2]]), "core")

    k0, l0, k3, l3 = keep(weights((0, 3), row_index, counts))
    k1, l1, k2, l2 = keep(weights((1, 2), row_index, counts))
    scaled_shape, words_t_shape = low_shape(CHUNK, COLUMNS), low_shape(384, CHUNK)
    g3, s3, t3, ctx_full, ctx_t = call(
        first_kernel, (piece_index,), (w3, c0, c1, k3, l3),
        [blocks_shape(4, low), scaled_shape, words_t_shape, low_shape(COLUMNS, 384), low_shape(384, COLUMNS)],
        WORDS_SCRATCH, CHUNK_FLOPS, 16,
    )

    def chunk(w, weight, log_count, dtype):
        return call(
            chunk_kernel, (), (w, weight, log_count, ctx_full, ctx_t),
            [blocks_shape(4, dtype), scaled_shape, words_t_shape], WORDS_SCRATCH, CHUNK_FLOPS, 16,
        )

    g1, s1, t1 = chunk(w1, k1, l1, low)
    g2, s2, t2 = chunk(w2, k2, l2, low)
    g0, s0, t0 = chunk(w0, k0, l0, f32)
    h_own, h_other = call(
        ctx_kernel, (result_index,), (s0, s1, s2, s3, t0, t1, t2, t3),
        [blocks_shape(8, f32), blocks_shape(8, low)],
        [pltpu.VMEM((384, COLUMNS), f32), pltpu.VMEM((COLUMNS, 384), f32)], 2 * CHUNK_FLOPS, 16,
    )

    f1 = go(g3, "core")
    ya = go(g2, "y")
    rn = go(jnp.concatenate([g1, f1]), "y")
    hc = go(h_other, "core")
    ya2 = go(ya, "y")
    s = h_own + hc.astype(f32)
    xa = go(s[6:].astype(low), "x")
    f2 = go(rn[4:], "core")
    z_own, z_next, z_far, z_back = call(
        sum_kernel, (), (g0, rn, f2, ya2),
        [jax.ShapeDtypeStruct((BLOCK, LO), f32)] * 2 + [low_shape(BLOCK, LO)] * 2, [], 4 * BLOCK * LO * 4, 8,
    )
    za, f3 = go(z_far, "z"), go(z_back, "core")
    (near_x,) = call(near_kernel, (), (s, xa, z_back), [blocks_shape(4, low)], [], 4 * BLOCK * LO * 2, 8)
    xr = go(near_x, "x")
    x4 = go(xr[2:], "core")
    rz = go(jnp.stack([(z_next + za.astype(f32)).astype(low), f3]), "z")
    t_own, t_far = call(
        last_kernel, (), (s, xr, x4), [jax.ShapeDtypeStruct((BLOCK, LO), f32), low_shape(BLOCK, LO)],
        [], 4 * BLOCK * LO, 8,
    )
    rl = go(t_far, "zl")
    f4 = go(rz[1], "core")

    word_scale = 2.0 / (counts.shape[1] * lax.axis_size("ctx"))
    ctx_scale = 2.0 / (counts.shape[0] * lax.axis_size("word"))
    new_ctx_vecs, new_ctx_bias, new_ctx_accum, new_ctx_bias_accum = update(
        t_own, rl, None, ctx_vecs, ctx_bias, ctx_accum, ctx_bias_accum, D - LO + 1, ctx_scale
    )
    new_word_vecs, new_word_bias, new_word_accum, new_word_bias_accum = update(
        z_own, rz, f4, word_vecs, word_bias, word_accum, word_bias_accum, D - LO, word_scale
    )
    return (
        new_word_vecs,
        new_word_bias,
        new_word_accum,
        new_word_bias_accum,
        new_ctx_vecs,
        new_ctx_bias,
        new_ctx_accum,
        new_ctx_bias_accum,
    )


def solution(mesh):
    words, contexts = P(("word", "ctx")), P(("ctx", "word"))
    return jax.shard_map(
        per_device,
        mesh=mesh,
        in_specs=(P("word", "ctx"), words, words, words, words, contexts, contexts, contexts, contexts),
        out_specs=(words, words, words, words, contexts, contexts, contexts, contexts),
        check_vma=False,
    )
```

```python
import functools
import math

import jax
import jax.numpy as jnp
from jax import lax
from jax.experimental import pallas as pl
from jax.experimental.pallas import tpu as pltpu
from jax.sharding import PartitionSpec as P


count_cap = 100.0
power_law = 0.75
step_rate = 0.2

ROWS = 96
BLOCK = 120
D = 300
LO = 256
USED = 320
MIB = 1 << 20


def pack_rows(main, tail):
    lane = lax.broadcasted_iota(jnp.int32, (24, 128), 1)
    low = lane < 64
    t = [tail[24 * g : 24 * g + 24, :] for g in range(4)]
    left = jnp.where(low, t[0], pltpu.roll(t[1], 64, 1))
    right = jnp.where(low, t[2], pltpu.roll(t[3], 64, 1))
    return jnp.concatenate([main, jnp.concatenate([left, right], axis=1)], axis=0)


def unpack_tail(packed):
    left, right = packed[ROWS:BLOCK, :128], packed[ROWS:BLOCK, 128:]
    return jnp.concatenate([left, pltpu.roll(left, 64, 1), right, pltpu.roll(right, 64, 1)], axis=0)


def to_column(row):
    eye = lax.broadcasted_iota(jnp.int32, (ROWS, ROWS), 0) == lax.broadcasted_iota(jnp.int32, (ROWS, ROWS), 1)
    return jnp.sum(jnp.where(eye, jnp.broadcast_to(row, (ROWS, ROWS)), 0.0), axis=1, keepdims=True)


def to_row(column):
    eye = lax.broadcasted_iota(jnp.int32, (ROWS, ROWS), 0) == lax.broadcasted_iota(jnp.int32, (ROWS, ROWS), 1)
    return jnp.sum(jnp.where(eye, jnp.broadcast_to(column, (ROWS, ROWS)), 0.0), axis=0, keepdims=True)


def pack_one(bias_lane, vec_ref, bias_ref, out_ref, tail_ref):
    tail_ref[...] = jnp.zeros_like(tail_ref)
    tail_ref[:, : D - LO] = vec_ref[:, LO:]
    lane = lax.broadcasted_iota(jnp.int32, (ROWS, 128), 1)
    tail = jnp.where(lane == bias_lane, jnp.broadcast_to(to_column(bias_ref[...]), (ROWS, 128)), tail_ref[...])
    out_ref[...] = pack_rows(vec_ref[:, :LO], tail).astype(jnp.bfloat16)


PIECES = (
    (0, 0, 0), (0, 0, 1), (1, 0, 0), (1, 0, 1), (0, -1, 0), (0, -1, 1), (1, -1, 0), (1, -1, 1), (0, 2, 0), (0, 2, 1),
    (1, 1, 0), (1, 1, 1), (0, 1, 0), (0, 1, 1), (1, 2, 0), (1, 2, 1),
)
RESULTS = tuple(
    (d, b, a) for d, b in ((0, 0), (0, 1), (0, -1), (0, 2), (1, 0), (1, -1), (1, 1), (1, 2)) for a in (0, 1)
)


def pack_kernel(wv, wb, cv, cb, word_out, ctx_out, row_index, piece_index, result_index, tail_ref):
    p, q = lax.axis_index("ctx"), lax.axis_index("word")
    y, z = lax.div(p, 4), lax.rem(p, 4)
    zl, x, c = lax.div(q, 8), lax.rem(lax.div(q, 2), 4), lax.rem(q, 2)
    s = 1 - 2 * c
    for k in range(4):
        for j in range(4):
            row_index[4 * k + j] = lax.rem(y + k * s + 4, 4) * 4 + lax.rem(z + j * s + 4, 4)
    for out, table in ((piece_index, PIECES), (result_index, RESULTS)):
        for i, (d, b, a) in enumerate(table):
            out[i] = lax.rem(zl + a, 2) * 8 + lax.rem(x + b * s + 4, 4) * 2 + lax.rem(c + d, 2)
    pack_one(D - LO, wv, wb, word_out, tail_ref)
    pack_one(D - LO + 1, cv, cb, ctx_out, tail_ref)


def pack(word_vecs, word_bias, ctx_vecs, ctx_bias):
    return pl.pallas_call(
        pack_kernel,
        out_specs=[pl.BlockSpec(memory_space=pltpu.VMEM)] * 2 + [pl.BlockSpec(memory_space=pltpu.SMEM)] * 3,
        out_shape=[jax.ShapeDtypeStruct((BLOCK, LO), jnp.bfloat16)] * 2 + [jax.ShapeDtypeStruct((16,), jnp.int32)] * 3,
        scratch_shapes=[pltpu.VMEM((ROWS, 128), jnp.float32)],
        compiler_params=pltpu.CompilerParams(vmem_limit_bytes=4 * MIB),
        cost_estimate=pl.CostEstimate(flops=100000, bytes_accessed=400000, transcendentals=0),
        name="pack",
    )(*(pltpu.with_memory_space_constraint(v, pltpu.HBM) for v in (word_vecs, word_bias.reshape(1, ROWS), ctx_vecs, ctx_bias.reshape(1, ROWS))))


def weight_kernel(chunks, index_ref, counts, *refs):
    outs, (held, sems) = refs[:-2], refs[-2:]

    def fetch(n):
        start = pl.multiple_of(index_ref[4 * chunks[n // 4] + n % 4] * ROWS, ROWS)
        return pltpu.make_async_copy(counts.at[pl.ds(start, ROWS)], held.at[n], sems.at[n])

    copies = [fetch(n) for n in range(4 * len(chunks))]
    for copy in copies:
        copy.start()
    for n, copy in enumerate(copies):
        weight_ref, log_ref = outs[n // 4 * 2], outs[n // 4 * 2 + 1]
        copy.wait()

        def step(i, _):
            rows = pl.ds(pl.multiple_of(i * 8, 8), 8)
            count = held[n, rows, :]
            log_count = jnp.log(jnp.maximum(count.astype(jnp.float32), 1.0))
            exponent = log_count * (power_law / math.log(2.0)) - power_law * math.log2(count_cap)
            power = jnp.exp2(jnp.minimum(exponent, 0.0))
            to = pl.ds(pl.multiple_of(n % 4 * ROWS + i * 8, 8), 8)
            weight_ref[to, :] = jnp.where(count > 0, power, 0.0)
            log_ref[to, :] = log_count
            return 0

        lax.fori_loop(0, ROWS // 8, step, 0, unroll=3)


def weights(chunks, index, counts):
    columns, n = counts.shape[1], len(chunks)
    return pl.pallas_call(
        functools.partial(weight_kernel, chunks),
        in_specs=[pl.BlockSpec(memory_space=pltpu.SMEM), pl.BlockSpec(memory_space=pltpu.HBM)],
        out_specs=[pl.BlockSpec(memory_space=pltpu.VMEM)] * (2 * n),
        out_shape=[pltpu.VMEM((4 * ROWS, columns), jnp.float32)] * (2 * n),
        scratch_shapes=[pltpu.VMEM((4 * n, ROWS, columns), jnp.int32), pltpu.SemaphoreType.DMA((4 * n,))],
        compiler_params=pltpu.CompilerParams(vmem_limit_bytes=8 * MIB),
        cost_estimate=pl.CostEstimate(
            flops=80 * n * ROWS * columns, bytes_accessed=48 * n * ROWS * columns, transcendentals=8 * n * ROWS * columns
        ),
    )(index, pltpu.with_memory_space_constraint(counts, pltpu.HBM))


def rows_of(index_ref, i):
    return pl.ds(pl.multiple_of(index_ref[i] * ROWS, ROWS), ROWS)


def word_chunk(blocks, weight, log_count, ctx_full, ctx_t, words, words_t, scaled_ref):
    lane = lax.broadcasted_iota(jnp.int32, (ROWS, 128), 1)
    bc = D - LO + 1
    for j in range(4):
        packed = blocks[j].astype(jnp.float32)
        tail = unpack_tail(packed)
        tail = jnp.where(lane < bc, tail, jnp.where(lane == bc, 1.0, 0.0))
        words[ROWS * j : ROWS * j + ROWS, :LO] = packed[:ROWS].astype(jnp.bfloat16)
        words[ROWS * j : ROWS * j + ROWS, LO:] = tail.astype(jnp.bfloat16)
    word_rows = words[...]
    words_t[...] = word_rows.T
    inner = jnp.dot(word_rows, ctx_t[...], preferred_element_type=jnp.float32)
    scaled_ref[...] = (weight[...] * (inner - log_count[...])).astype(jnp.bfloat16)
    term = jnp.dot(scaled_ref[...], ctx_full[...], preferred_element_type=jnp.float32)
    parts = [term[ROWS * j : ROWS * j + ROWS] for j in range(4)]
    return [pack_rows(part[:, :LO], part[:, LO:]) for part in parts]


def build(index_ref, c0, c1, ctx_full, ctx_t):
    lane = lax.broadcasted_iota(jnp.int32, (ROWS, 128), 1)
    bw, bc = D - LO, D - LO + 1
    for i in range(16):
        packed = (c0[i] if i < 10 else c1[i - 10]).astype(jnp.float32)
        tail = unpack_tail(packed)
        tail = jnp.where(lane == bw, 1.0, jnp.where(lane <= bc, tail, 0.0))
        ctx_full[rows_of(index_ref, i), :LO] = packed[:ROWS].astype(jnp.bfloat16)
        ctx_full[rows_of(index_ref, i), LO:] = tail.astype(jnp.bfloat16)
    ctx_t[...] = ctx_full[...].T


def chunk_kernel(w, weight, log_count, ctx_full, ctx_t, grad, scaled, words_t, words):
    blocks = [w[j] for j in range(4)]
    for j, packed in enumerate(word_chunk(blocks, weight, log_count, ctx_full, ctx_t, words, words_t, scaled)):
        grad[j] = packed.astype(grad.dtype)


def first_kernel(index_ref, w, c0, c1, weight, log_count, grad, scaled, words_t, ctx_full, ctx_t, words):
    build(index_ref, c0, c1, ctx_full, ctx_t)
    chunk_kernel(w, weight, log_count, ctx_full, ctx_t, grad, scaled, words_t, words)


def ctx_kernel(index_ref, s0, s1, s2, s3, t0, t1, t2, t3, h_own, h_other, ctx_grad, back):
    for k, (t, s) in enumerate(((t0, s0), (t1, s1), (t2, s2), (t3, s3))):
        term = jnp.dot(t[:USED, :], s[...], preferred_element_type=jnp.float32)
        ctx_grad[:USED, :] = term if k == 0 else ctx_grad[:USED, :] + term
    back[...] = ctx_grad[...].T
    for i in range(16):
        term = back[rows_of(index_ref, i), :]
        packed = pack_rows(term[:, :LO], term[:, LO:])
        if i < 8:
            h_own[i] = packed
        else:
            h_other[i - 8] = packed.astype(jnp.bfloat16)


def sum_kernel(g0, rn, f2, ya, own, nxt, far, back):
    f32 = jnp.float32
    for j, out in enumerate((own, nxt, far, back)):
        total = g0[j] + rn[j].astype(f32) + f2[j].astype(f32) + ya[j].astype(f32)
        out[...] = total.astype(out.dtype)


def join_kernel(a, b, c, out):
    for j, ref in enumerate((a, b, c)):
        out[j] = ref[...]


def near_kernel(s, xa, _, out):
    for j in range(2):
        out[j] = (s[2 + j] + xa[j].astype(jnp.float32)).astype(jnp.bfloat16)


def last_kernel(s, xr, xb, own, far):
    for j, out in enumerate((own, far)):
        out[...] = (s[j] + xr[j].astype(jnp.float32) + xb[j].astype(jnp.float32)).astype(out.dtype)


CHUNK, COLUMNS = 4 * ROWS, 16 * ROWS
SMEM_SPEC = pl.BlockSpec(memory_space=pltpu.SMEM)
VMEM_SPEC = pl.BlockSpec(memory_space=pltpu.VMEM)


def blocks_shape(n, dtype):
    return jax.ShapeDtypeStruct((n, BLOCK, LO), dtype)


def low_shape(*dims):
    return jax.ShapeDtypeStruct(dims, jnp.bfloat16)


def call(kernel, scalars, operands, out_shape, scratch, flops, limit):
    return pl.pallas_call(
        kernel,
        in_specs=[SMEM_SPEC] * len(scalars) + [VMEM_SPEC] * len(operands),
        out_specs=[VMEM_SPEC] * len(out_shape),
        out_shape=out_shape,
        scratch_shapes=scratch,
        compiler_params=pltpu.CompilerParams(vmem_limit_bytes=limit * MIB),
        cost_estimate=pl.CostEstimate(flops=flops, bytes_accessed=4 * MIB, transcendentals=0),
    )(*scalars, *operands)


CHUNK_FLOPS = 4 * CHUNK * COLUMNS * 384
WORDS_SCRATCH = [pltpu.VMEM((CHUNK, 384), jnp.bfloat16)]


def update_kernel(bias_lane, scale, total_ref, add_a, add_b, vec_ref, bias_ref, acc_ref, bacc_ref, nv, nb, na, nba):
    packed = total_ref[...] + add_a[...].astype(jnp.float32)
    if add_b is not None:
        packed = packed + add_b[...].astype(jnp.float32)
    packed = packed * scale
    tail = unpack_tail(packed)
    for columns, grad in ((slice(0, LO), packed[:ROWS]), (slice(LO, D), tail[:, : D - LO])):
        accum = acc_ref[:, columns] + grad * grad
        na[:, columns] = accum
        nv[:, columns] = vec_ref[:, columns] - step_rate * grad / jnp.sqrt(accum)
    grad = to_row(tail[:, bias_lane : bias_lane + 1])
    accum = bacc_ref[...] + grad * grad
    nba[...] = accum
    nb[...] = bias_ref[...] - step_rate * grad / jnp.sqrt(accum)


def update(total, add_a, add_b, vecs, bias, accum, bias_accum, bias_lane, scale):
    row = lambda a: a.reshape(1, ROWS)
    if add_b is None:
        kernel = lambda t, a, *rest: update_kernel(bias_lane, scale, t, a, None, *rest)
        sums = (total, add_a)
    else:
        kernel = functools.partial(update_kernel, bias_lane, scale)
        sums = (total, add_a, add_b)
    f32 = jnp.float32
    nv, nb, na, nba = pl.pallas_call(
        kernel,
        out_shape=[
            jax.ShapeDtypeStruct((ROWS, D), f32),
            jax.ShapeDtypeStruct((1, ROWS), f32),
            jax.ShapeDtypeStruct((ROWS, D), f32),
            jax.ShapeDtypeStruct((1, ROWS), f32),
        ],
        compiler_params=pltpu.CompilerParams(vmem_limit_bytes=6 * MIB),
        cost_estimate=pl.CostEstimate(flops=400000, bytes_accessed=800000, transcendentals=30000),
    )(*sums, vecs, row(bias), accum, row(bias_accum))
    return nv, nb.reshape(ROWS), na, nba.reshape(ROWS)


def spread(index):
    q, p = index // 16, index % 16
    return q // 8, q // 2 % 4, q % 2, p // 4, p % 4


def place(zl, x, c, y, z):
    return (zl % 2 * 8 + x % 4 * 2 + c % 2) * 16 + y % 4 * 4 + z % 4


def move(value, axis):
    perm = []
    for i in range(256):
        zl, x, c, y, z = spread(i)
        s = 1 - 2 * c
        to = {
            "core": (zl, x, c + 1, y, z),
            "zl": (zl + 1, x, c, y, z),
            "x": (zl, x + s, c, y, z),
            "y": (zl, x, c, y + s, z),
            "z": (zl, x, c, y, z + s),
            "x back": (zl, x - s, c, y, z),
            "z back": (zl, x, c, y, z - s),
            "z back, core": (zl, x, c + 1, y, z - s),
        }[axis]
        perm.append((i, place(*to)))
    return lax.ppermute(value, ("word", "ctx"), perm)


def keep(arrays):
    return [pltpu.with_memory_space_constraint(v, pltpu.VMEM) for v in arrays]


def per_device(
    counts,
    word_vecs,
    word_bias,
    word_accum,
    word_bias_accum,
    ctx_vecs,
    ctx_bias,
    ctx_accum,
    ctx_bias_accum,
):
    f32, low = jnp.float32, jnp.bfloat16
    go = lambda value, axis: move(value, axis)

    word_block, ctx_block, row_index, piece_index, result_index = pack(word_vecs, word_bias, ctx_vecs, ctx_bias)

    both = jnp.stack([word_block, go(word_block, "core")])
    pair = jnp.stack([ctx_block, go(ctx_block, "zl")])
    zr1a, zr1b = go(word_block, "z"), go(word_block, "z back, core")
    zr1 = jnp.stack([zr1a, zr1b])
    y1a = go(both, "y")
    four = jnp.concatenate([pair, go(pair, "core")])
    zr2 = go(zr1a, "z")
    xr1 = go(four, "x")
    y1b = go(zr1, "y")
    (joined,) = call(join_kernel, (), (zr1b, zr1a, zr2), [blocks_shape(3, low)], [], 3 * BLOCK * LO, 4)
    zr2 = zr2[None]
    e1 = go(joined, "core")
    y1c = go(jnp.concatenate([e1, zr2]), "y")
    xr2 = go(xr1[:2], "x")
    c0 = jnp.concatenate([four, xr1, xr2])
    c1 = go(c0[4:], "core")
    w0 = jnp.concatenate([both[:1], e1[:1], zr2, zr1[:1]])
    w3 = jnp.concatenate([y1a[:1], y1c[:1], y1c[3:], y1b[:1]])
    w2 = go(w3, "y")
    w1 = go(jnp.concatenate([y1a[1:], y1b[1:], y1c[2:3], y1c[1:2]]), "core")

    k0, l0, k3, l3 = keep(weights((0, 3), row_index, counts))
    k1, l1, k2, l2 = keep(weights((1, 2), row_index, counts))
    scaled_shape, words_t_shape = low_shape(CHUNK, COLUMNS), low_shape(384, CHUNK)
    g3, s3, t3, ctx_full, ctx_t = call(
        first_kernel, (piece_index,), (w3, c0, c1, k3, l3),
        [blocks_shape(4, low), scaled_shape, words_t_shape, low_shape(COLUMNS, 384), low_shape(384, COLUMNS)],
        WORDS_SCRATCH, CHUNK_FLOPS, 16,
    )

    def chunk(w, weight, log_count, dtype):
        return call(
            chunk_kernel, (), (w, weight, log_count, ctx_full, ctx_t),
            [blocks_shape(4, dtype), scaled_shape, words_t_shape], WORDS_SCRATCH, CHUNK_FLOPS, 16,
        )

    g1, s1, t1 = chunk(w1, k1, l1, low)
    g2, s2, t2 = chunk(w2, k2, l2, low)
    g0, s0, t0 = chunk(w0, k0, l0, f32)
    h_own, h_other = call(
        ctx_kernel, (result_index,), (s0, s1, s2, s3, t0, t1, t2, t3),
        [blocks_shape(8, f32), blocks_shape(8, low)],
        [pltpu.VMEM((384, COLUMNS), f32), pltpu.VMEM((COLUMNS, 384), f32)], 2 * CHUNK_FLOPS, 16,
    )

    f1 = go(g3, "core")
    ya = go(g2, "y")
    rn = go(jnp.concatenate([g1, f1]), "y")
    hc = go(h_other, "core")
    ya2 = go(ya, "y")
    s = h_own + hc.astype(f32)
    xa, xb = go(s[6:].astype(low), "x"), go(s[4:6].astype(low), "x back")
    f2 = go(rn[4:], "core")
    z_own, z_next, z_far, z_back = call(
        sum_kernel, (), (g0, rn, f2, ya2),
        [jax.ShapeDtypeStruct((BLOCK, LO), f32)] * 2 + [low_shape(BLOCK, LO)] * 2, [], 4 * BLOCK * LO * 4, 8,
    )
    za, rzb = go(z_far, "z"), go(z_back, "z back")
    (near_x,) = call(near_kernel, (), (s, xa, z_back), [blocks_shape(2, low)], [], 2 * BLOCK * LO * 2, 8)
    xr = go(near_x, "x")
    rza = go((z_next + za.astype(f32)).astype(low), "z")
    t_own, t_far = call(
        last_kernel, (), (s, xr, xb), [jax.ShapeDtypeStruct((BLOCK, LO), f32), low_shape(BLOCK, LO)],
        [], 4 * BLOCK * LO, 8,
    )
    rl = go(t_far, "zl")

    word_scale = 2.0 / (counts.shape[1] * lax.axis_size("ctx"))
    ctx_scale = 2.0 / (counts.shape[0] * lax.axis_size("word"))
    new_ctx_vecs, new_ctx_bias, new_ctx_accum, new_ctx_bias_accum = update(
        t_own, rl, None, ctx_vecs, ctx_bias, ctx_accum, ctx_bias_accum, D - LO + 1, ctx_scale
    )
    new_word_vecs, new_word_bias, new_word_accum, new_word_bias_accum = update(
        z_own, rza, rzb, word_vecs, word_bias, word_accum, word_bias_accum, D - LO, word_scale
    )
    return (
        new_word_vecs,
        new_word_bias,
        new_word_accum,
        new_word_bias_accum,
        new_ctx_vecs,
        new_ctx_bias,
        new_ctx_accum,
        new_ctx_bias_accum,
    )


def solution(mesh):
    words, contexts = P(("word", "ctx")), P(("ctx", "word"))
    return jax.shard_map(
        per_device,
        mesh=mesh,
        in_specs=(P("word", "ctx"), words, words, words, words, contexts, contexts, contexts, contexts),
        out_specs=(words, words, words, words, contexts, contexts, contexts, contexts),
        check_vma=False,
    )
```

```python
import functools
import math

import jax
import jax.numpy as jnp
from jax import lax
from jax.experimental import pallas as pl
from jax.experimental.pallas import tpu as pltpu
from jax.sharding import PartitionSpec as P


count_cap = 100.0
power_law = 0.75
step_rate = 0.2

ROWS = 96
BLOCK = 120
D = 300
LO = 256
USED = 320
MIB = 1 << 20


def pack_rows(main, tail):
    lane = lax.broadcasted_iota(jnp.int32, (24, 128), 1)
    low = lane < 64
    t = [tail[24 * g : 24 * g + 24, :] for g in range(4)]
    left = jnp.where(low, t[0], pltpu.roll(t[1], 64, 1))
    right = jnp.where(low, t[2], pltpu.roll(t[3], 64, 1))
    return jnp.concatenate([main, jnp.concatenate([left, right], axis=1)], axis=0)


def unpack_tail(packed):
    left, right = packed[ROWS:BLOCK, :128], packed[ROWS:BLOCK, 128:]
    return jnp.concatenate([left, pltpu.roll(left, 64, 1), right, pltpu.roll(right, 64, 1)], axis=0)


def to_column(row):
    eye = lax.broadcasted_iota(jnp.int32, (ROWS, ROWS), 0) == lax.broadcasted_iota(jnp.int32, (ROWS, ROWS), 1)
    return jnp.sum(jnp.where(eye, jnp.broadcast_to(row, (ROWS, ROWS)), 0.0), axis=1, keepdims=True)


def to_row(column):
    eye = lax.broadcasted_iota(jnp.int32, (ROWS, ROWS), 0) == lax.broadcasted_iota(jnp.int32, (ROWS, ROWS), 1)
    return jnp.sum(jnp.where(eye, jnp.broadcast_to(column, (ROWS, ROWS)), 0.0), axis=0, keepdims=True)


def pack_one(bias_lane, vec_ref, bias_ref, out_ref, tail_ref):
    tail_ref[...] = jnp.zeros_like(tail_ref)
    tail_ref[:, : D - LO] = vec_ref[:, LO:]
    lane = lax.broadcasted_iota(jnp.int32, (ROWS, 128), 1)
    tail = jnp.where(lane == bias_lane, jnp.broadcast_to(to_column(bias_ref[...]), (ROWS, 128)), tail_ref[...])
    out_ref[...] = pack_rows(vec_ref[:, :LO], tail).astype(jnp.bfloat16)


PIECES = (
    (0, 0, 0), (0, 0, 1), (1, 0, 0), (1, 0, 1), (0, -1, 0), (0, -1, 1), (1, -1, 0), (1, -1, 1), (0, 2, 0), (0, 2, 1),
    (1, 1, 0), (1, 1, 1), (0, 1, 0), (0, 1, 1), (1, 2, 0), (1, 2, 1),
)
RESULTS = tuple(
    (d, b, a) for d, b in ((0, 0), (0, 1), (0, -1), (0, 2), (1, 0), (1, -1), (1, 1), (1, 2)) for a in (0, 1)
)


def pack_kernel(wv, wb, cv, cb, word_out, ctx_out, row_index, piece_index, result_index, tail_ref):
    p, q = lax.axis_index("ctx"), lax.axis_index("word")
    y, z = lax.div(p, 4), lax.rem(p, 4)
    zl, x, c = lax.div(q, 8), lax.rem(lax.div(q, 2), 4), lax.rem(q, 2)
    s = 1 - 2 * c
    for k in range(4):
        for j in range(4):
            row_index[4 * k + j] = lax.rem(y + k * s + 4, 4) * 4 + lax.rem(z + j * s + 4, 4)
    for out, table in ((piece_index, PIECES), (result_index, RESULTS)):
        for i, (d, b, a) in enumerate(table):
            out[i] = lax.rem(zl + a, 2) * 8 + lax.rem(x + b * s + 4, 4) * 2 + lax.rem(c + d, 2)
    pack_one(D - LO, wv, wb, word_out, tail_ref)
    pack_one(D - LO + 1, cv, cb, ctx_out, tail_ref)


def pack(word_vecs, word_bias, ctx_vecs, ctx_bias):
    return pl.pallas_call(
        pack_kernel,
        out_specs=[pl.BlockSpec(memory_space=pltpu.VMEM)] * 2 + [pl.BlockSpec(memory_space=pltpu.SMEM)] * 3,
        out_shape=[jax.ShapeDtypeStruct((BLOCK, LO), jnp.bfloat16)] * 2 + [jax.ShapeDtypeStruct((16,), jnp.int32)] * 3,
        scratch_shapes=[pltpu.VMEM((ROWS, 128), jnp.float32)],
        compiler_params=pltpu.CompilerParams(vmem_limit_bytes=4 * MIB),
        cost_estimate=pl.CostEstimate(flops=100000, bytes_accessed=400000, transcendentals=0),
        name="pack",
    )(*(pltpu.with_memory_space_constraint(v, pltpu.HBM) for v in (word_vecs, word_bias.reshape(1, ROWS), ctx_vecs, ctx_bias.reshape(1, ROWS))))


AHEAD = 3


def weight_kernel(chunks, index_ref, counts, *refs):
    outs, (held, sems) = refs[:-2], refs[-2:]

    def fetch(n):
        start = pl.multiple_of(index_ref[4 * chunks[n // 4] + n % 4] * ROWS, ROWS)
        return pltpu.make_async_copy(counts.at[pl.ds(start, ROWS)], held.at[n], sems.at[n])

    copies = [fetch(n) for n in range(4 * len(chunks))]
    for copy in copies[:AHEAD]:
        copy.start()
    for n, copy in enumerate(copies):
        weight_ref, log_ref = outs[n // 4 * 2], outs[n // 4 * 2 + 1]
        copy.wait()
        if n + AHEAD < len(copies):
            copies[n + AHEAD].start()

        def step(i, _):
            rows = pl.ds(pl.multiple_of(i * 8, 8), 8)
            count = held[n, rows, :]
            log_count = jnp.log(jnp.maximum(count.astype(jnp.float32), 1.0))
            exponent = log_count * (power_law / math.log(2.0)) - power_law * math.log2(count_cap)
            power = jnp.exp2(jnp.minimum(exponent, 0.0))
            to = pl.ds(pl.multiple_of(n % 4 * ROWS + i * 8, 8), 8)
            weight_ref[to, :] = jnp.where(count > 0, power, 0.0)
            log_ref[to, :] = log_count
            return 0

        lax.fori_loop(0, ROWS // 8, step, 0, unroll=3)


def weights(chunks, index, counts):
    columns, n = counts.shape[1], len(chunks)
    return pl.pallas_call(
        functools.partial(weight_kernel, chunks),
        in_specs=[pl.BlockSpec(memory_space=pltpu.SMEM), pl.BlockSpec(memory_space=pltpu.HBM)],
        out_specs=[pl.BlockSpec(memory_space=pltpu.VMEM)] * (2 * n),
        out_shape=[pltpu.VMEM((4 * ROWS, columns), jnp.float32)] * (2 * n),
        scratch_shapes=[pltpu.VMEM((4 * n, ROWS, columns), jnp.int32), pltpu.SemaphoreType.DMA((4 * n,))],
        compiler_params=pltpu.CompilerParams(vmem_limit_bytes=8 * MIB),
        cost_estimate=pl.CostEstimate(
            flops=80 * n * ROWS * columns, bytes_accessed=48 * n * ROWS * columns, transcendentals=8 * n * ROWS * columns
        ),
    )(index, pltpu.with_memory_space_constraint(counts, pltpu.HBM))


def rows_of(index_ref, i):
    return pl.ds(pl.multiple_of(index_ref[i] * ROWS, ROWS), ROWS)


def word_chunk(blocks, weight, log_count, ctx_full, ctx_t, words, words_t, scaled_ref):
    lane = lax.broadcasted_iota(jnp.int32, (ROWS, 128), 1)
    bc = D - LO + 1
    for j in range(4):
        packed = blocks[j].astype(jnp.float32)
        tail = unpack_tail(packed)
        tail = jnp.where(lane < bc, tail, jnp.where(lane == bc, 1.0, 0.0))
        words[ROWS * j : ROWS * j + ROWS, :LO] = packed[:ROWS].astype(jnp.bfloat16)
        words[ROWS * j : ROWS * j + ROWS, LO:] = tail.astype(jnp.bfloat16)
    word_rows = words[...]
    words_t[...] = word_rows.T
    inner = jnp.dot(word_rows, ctx_t[...], preferred_element_type=jnp.float32)
    scaled_ref[...] = (weight[...] * (inner - log_count[...])).astype(jnp.bfloat16)
    term = jnp.dot(scaled_ref[...], ctx_full[...], preferred_element_type=jnp.float32)
    parts = [term[ROWS * j : ROWS * j + ROWS] for j in range(4)]
    return [pack_rows(part[:, :LO], part[:, LO:]) for part in parts]


def build(index_ref, c0, c1, ctx_full, ctx_t):
    lane = lax.broadcasted_iota(jnp.int32, (ROWS, 128), 1)
    bw, bc = D - LO, D - LO + 1
    for i in range(16):
        packed = (c0[i] if i < 10 else c1[i - 10]).astype(jnp.float32)
        tail = unpack_tail(packed)
        tail = jnp.where(lane == bw, 1.0, jnp.where(lane <= bc, tail, 0.0))
        ctx_full[rows_of(index_ref, i), :LO] = packed[:ROWS].astype(jnp.bfloat16)
        ctx_full[rows_of(index_ref, i), LO:] = tail.astype(jnp.bfloat16)
    ctx_t[...] = ctx_full[...].T


def chunk_kernel(w, weight, log_count, ctx_full, ctx_t, grad, scaled, words_t, words):
    blocks = [w[j] for j in range(4)]
    for j, packed in enumerate(word_chunk(blocks, weight, log_count, ctx_full, ctx_t, words, words_t, scaled)):
        grad[j] = packed.astype(grad.dtype)


def first_kernel(index_ref, w, c0, c1, weight, log_count, grad, scaled, words_t, ctx_full, ctx_t, words):
    build(index_ref, c0, c1, ctx_full, ctx_t)
    chunk_kernel(w, weight, log_count, ctx_full, ctx_t, grad, scaled, words_t, words)


def ctx_kernel(index_ref, s0, s1, s2, s3, t0, t1, t2, t3, h_own, h_other, ctx_grad, back):
    for k, (t, s) in enumerate(((t0, s0), (t1, s1), (t2, s2), (t3, s3))):
        term = jnp.dot(t[:USED, :], s[...], preferred_element_type=jnp.float32)
        ctx_grad[:USED, :] = term if k == 0 else ctx_grad[:USED, :] + term
    back[...] = ctx_grad[...].T
    for i in range(16):
        term = back[rows_of(index_ref, i), :]
        packed = pack_rows(term[:, :LO], term[:, LO:])
        if i < 8:
            h_own[i] = packed
        else:
            h_other[i - 8] = packed.astype(jnp.bfloat16)


def sum_kernel(g0, rn, f2, ya, own, nxt, far, back):
    f32 = jnp.float32
    for j, out in enumerate((own, nxt, far, back)):
        total = g0[j] + rn[j].astype(f32) + f2[j].astype(f32) + ya[j].astype(f32)
        out[...] = total.astype(out.dtype)


def join_kernel(a, b, c, out):
    for j, ref in enumerate((a, b, c)):
        out[j] = ref[...]


def near_kernel(s, xa, _, out):
    for j in range(2):
        out[j] = (s[2 + j] + xa[j].astype(jnp.float32)).astype(jnp.bfloat16)


def last_kernel(s, xr, xb, own, far):
    for j, out in enumerate((own, far)):
        out[...] = (s[j] + xr[j].astype(jnp.float32) + xb[j].astype(jnp.float32)).astype(out.dtype)


CHUNK, COLUMNS = 4 * ROWS, 16 * ROWS
SMEM_SPEC = pl.BlockSpec(memory_space=pltpu.SMEM)
VMEM_SPEC = pl.BlockSpec(memory_space=pltpu.VMEM)


def blocks_shape(n, dtype):
    return jax.ShapeDtypeStruct((n, BLOCK, LO), dtype)


def low_shape(*dims):
    return jax.ShapeDtypeStruct(dims, jnp.bfloat16)


def call(kernel, scalars, operands, out_shape, scratch, flops, limit):
    return pl.pallas_call(
        kernel,
        in_specs=[SMEM_SPEC] * len(scalars) + [VMEM_SPEC] * len(operands),
        out_specs=[VMEM_SPEC] * len(out_shape),
        out_shape=out_shape,
        scratch_shapes=scratch,
        compiler_params=pltpu.CompilerParams(vmem_limit_bytes=limit * MIB),
        cost_estimate=pl.CostEstimate(flops=flops, bytes_accessed=4 * MIB, transcendentals=0),
    )(*scalars, *operands)


CHUNK_FLOPS = 4 * CHUNK * COLUMNS * 384
WORDS_SCRATCH = [pltpu.VMEM((CHUNK, 384), jnp.bfloat16)]


def update_one(bias_lane, scale, sums, params, outs):
    vec_ref, bias_ref, acc_ref, bacc_ref = params
    nv, nb, na, nba = outs
    packed = sums[0][...]
    for ref in sums[1:]:
        packed = packed + ref[...].astype(jnp.float32)
    packed = packed * scale
    tail = unpack_tail(packed)
    for columns, grad in ((slice(0, LO), packed[:ROWS]), (slice(LO, D), tail[:, : D - LO])):
        accum = acc_ref[:, columns] + grad * grad
        na[:, columns] = accum
        nv[:, columns] = vec_ref[:, columns] - step_rate * grad / jnp.sqrt(accum)
    grad = to_row(tail[:, bias_lane : bias_lane + 1])
    accum = bacc_ref[...] + grad * grad
    nba[...] = accum
    nb[...] = bias_ref[...] - step_rate * grad / jnp.sqrt(accum)


def update(word_sums, word_params, word_scale, ctx_sums, ctx_params, ctx_scale):
    def kernel(*refs):
        words, refs = refs[:3], refs[3:]
        contexts, refs = refs[:2], refs[2:]
        update_one(D - LO, word_scale, words, refs[:4], refs[8:12])
        update_one(D - LO + 1, ctx_scale, contexts, refs[4:8], refs[12:16])

    row = lambda a: a.reshape(1, ROWS) if a.ndim == 1 else a
    shapes = [jax.ShapeDtypeStruct((ROWS, D), jnp.float32), jax.ShapeDtypeStruct((1, ROWS), jnp.float32)]
    outs = pl.pallas_call(
        kernel,
        out_shape=shapes * 4,
        compiler_params=pltpu.CompilerParams(vmem_limit_bytes=8 * MIB),
        cost_estimate=pl.CostEstimate(flops=800000, bytes_accessed=1600000, transcendentals=60000),
        name="update",
    )(*word_sums, *ctx_sums, *(row(a) for a in (*word_params, *ctx_params)))
    return tuple(a.reshape(ROWS) if a.shape[0] == 1 else a for a in outs)


def spread(index):
    q, p = index // 16, index % 16
    return q // 8, q // 2 % 4, q % 2, p // 4, p % 4


def place(zl, x, c, y, z):
    return (zl % 2 * 8 + x % 4 * 2 + c % 2) * 16 + y % 4 * 4 + z % 4


def move(value, axis):
    perm = []
    for i in range(256):
        zl, x, c, y, z = spread(i)
        s = 1 - 2 * c
        to = {
            "core": (zl, x, c + 1, y, z),
            "zl": (zl + 1, x, c, y, z),
            "x": (zl, x + s, c, y, z),
            "y": (zl, x, c, y + s, z),
            "z": (zl, x, c, y, z + s),
            "x back": (zl, x - s, c, y, z),
            "z back": (zl, x, c, y, z - s),
            "z back, core": (zl, x, c + 1, y, z - s),
        }[axis]
        perm.append((i, place(*to)))
    return lax.ppermute(value, ("word", "ctx"), perm)


def keep(arrays):
    return [pltpu.with_memory_space_constraint(v, pltpu.VMEM) for v in arrays]


def per_device(
    counts,
    word_vecs,
    word_bias,
    word_accum,
    word_bias_accum,
    ctx_vecs,
    ctx_bias,
    ctx_accum,
    ctx_bias_accum,
):
    f32, low = jnp.float32, jnp.bfloat16
    go = lambda value, axis: move(value, axis)

    word_block, ctx_block, row_index, piece_index, result_index = pack(word_vecs, word_bias, ctx_vecs, ctx_bias)

    both = jnp.stack([word_block, go(word_block, "core")])
    pair = jnp.stack([ctx_block, go(ctx_block, "zl")])
    zr1a, zr1b = go(word_block, "z"), go(word_block, "z back, core")
    zr1 = jnp.stack([zr1a, zr1b])
    y1a = go(both, "y")
    four = jnp.concatenate([pair, go(pair, "core")])
    zr2 = go(zr1a, "z")
    xr1 = go(four, "x")
    y1b = go(zr1, "y")
    (joined,) = call(join_kernel, (), (zr1b, zr1a, zr2), [blocks_shape(3, low)], [], 3 * BLOCK * LO, 4)
    zr2 = zr2[None]
    e1 = go(joined, "core")
    y1c = go(jnp.concatenate([e1, zr2]), "y")
    xr2 = go(xr1[:2], "x")
    c0 = jnp.concatenate([four, xr1, xr2])
    c1 = go(c0[4:], "core")
    w0 = jnp.concatenate([both[:1], e1[:1], zr2, zr1[:1]])
    w3 = jnp.concatenate([y1a[:1], y1c[:1], y1c[3:], y1b[:1]])
    w2 = go(w3, "y")
    w1 = go(jnp.concatenate([y1a[1:], y1b[1:], y1c[2:3], y1c[1:2]]), "core")

    k0, l0, k3, l3 = keep(weights((0, 3), row_index, counts))
    k1, l1, k2, l2 = keep(weights((1, 2), row_index, counts))
    scaled_shape, words_t_shape = low_shape(CHUNK, COLUMNS), low_shape(384, CHUNK)
    g3, s3, t3, ctx_full, ctx_t = call(
        first_kernel, (piece_index,), (w3, c0, c1, k3, l3),
        [blocks_shape(4, low), scaled_shape, words_t_shape, low_shape(COLUMNS, 384), low_shape(384, COLUMNS)],
        WORDS_SCRATCH, CHUNK_FLOPS, 16,
    )

    def chunk(w, weight, log_count, dtype):
        return call(
            chunk_kernel, (), (w, weight, log_count, ctx_full, ctx_t),
            [blocks_shape(4, dtype), scaled_shape, words_t_shape], WORDS_SCRATCH, CHUNK_FLOPS, 16,
        )

    g1, s1, t1 = chunk(w1, k1, l1, low)
    g2, s2, t2 = chunk(w2, k2, l2, low)
    g0, s0, t0 = chunk(w0, k0, l0, f32)
    h_own, h_other = call(
        ctx_kernel, (result_index,), (s0, s1, s2, s3, t0, t1, t2, t3),
        [blocks_shape(8, f32), blocks_shape(8, low)],
        [pltpu.VMEM((384, COLUMNS), f32), pltpu.VMEM((COLUMNS, 384), f32)], 2 * CHUNK_FLOPS, 16,
    )

    f1 = go(g3, "core")
    ya = go(g2, "y")
    rn = go(jnp.concatenate([g1, f1]), "y")
    hc = go(h_other, "core")
    ya2 = go(ya, "y")
    s = h_own + hc.astype(f32)
    xa, xb = go(s[6:].astype(low), "x"), go(s[4:6].astype(low), "x back")
    f2 = go(rn[4:], "core")
    z_own, z_next, z_far, z_back = call(
        sum_kernel, (), (g0, rn, f2, ya2),
        [jax.ShapeDtypeStruct((BLOCK, LO), f32)] * 2 + [low_shape(BLOCK, LO)] * 2, [], 4 * BLOCK * LO * 4, 8,
    )
    za, rzb = go(z_far, "z"), go(z_back, "z back")
    (near_x,) = call(near_kernel, (), (s, xa, z_back), [blocks_shape(2, low)], [], 2 * BLOCK * LO * 2, 8)
    xr = go(near_x, "x")
    rza = go((z_next + za.astype(f32)).astype(low), "z")
    t_own, t_far = call(
        last_kernel, (), (s, xr, xb), [jax.ShapeDtypeStruct((BLOCK, LO), f32), low_shape(BLOCK, LO)],
        [], 4 * BLOCK * LO, 8,
    )
    rl = go(t_far, "zl")

    word_scale = 2.0 / (counts.shape[1] * lax.axis_size("ctx"))
    ctx_scale = 2.0 / (counts.shape[0] * lax.axis_size("word"))
    return update(
        (z_own, rza, rzb), (word_vecs, word_bias, word_accum, word_bias_accum), word_scale,
        (t_own, rl), (ctx_vecs, ctx_bias, ctx_accum, ctx_bias_accum), ctx_scale,
    )


def solution(mesh):
    words, contexts = P(("word", "ctx")), P(("ctx", "word"))
    return jax.shard_map(
        per_device,
        mesh=mesh,
        in_specs=(P("word", "ctx"), words, words, words, words, contexts, contexts, contexts, contexts),
        out_specs=(words, words, words, words, contexts, contexts, contexts, contexts),
        check_vma=False,
    )
```
